32 devices in a mesh: slab: 8 (over y, x, core), coil: 4 (over z).
Axes of the slice: x: 2, y: 2, z: 4, core: 2. Of those that a mesh axis runs over, the one named last changes fastest.
Arguments:
- sensitivity: float32 [4, 2, 16, 256, 128], P('coil', None, 'slab'), may hold values from -4 to 4
- kspace: float32 [4, 2, 16, 256, 128], P('coil', None, 'slab')
- sampling: int32 [16, 256, 128], P('slab'), may hold values 0 or 1
- prior_image: float32 [2, 16, 256, 128], P(None, 'slab', 'coil')
- w_first: bfloat16 [32, 2, 3, 3, 3], replicated, may hold values from -0.875 to 0.875
- w_middle: bfloat16 [3, 32, 32, 3, 3, 3], replicated, may hold values from -0.21875 to 0.21875
- w_last: bfloat16 [2, 32, 3, 3, 3], replicated, may hold values from -0.21875 to 0.21875
Outputs:
- solution: float32 [2, 16, 256, 128], P(None, 'slab', 'coil')
- refined: float32 [2, 16, 256, 128], P(None, 'slab', 'coil')
The draws below stay inside these ranges and needn't reach their ends.
Inputs may be any that keep to these rules, and one draw needn't show every extreme that they name: sampling marks the measured ky-kz positions of each readout plane.
All inputs are finite; a program needn't handle non-finite values. No bound on the sum of `sampling` on one device may be relied on, other than what follows from the above.
Results may differ from the reference program's by a relative error of at most 0.0015.
Values may be sent and summed in bfloat16 or wider, within the bound.
A program may use at most 128 MiB of HBM per device.

```python
import math
import jax
import jax.numpy as jnp
from jax import lax

NY = 256
NZ = 128
CHANNELS = 32
LAYERS = 5
ITERS = 2
NX = 16
COILS = 4


def scaled_field(key, lead_shape):
    full_shape = lead_shape + (NX, NY, NZ)
    key_values, key_rows, key_columns = jax.random.split(key, 3)
    positions = jnp.arange(NX, dtype=jnp.float32) / max(NX - 1, 1)
    values_raw = jax.random.truncated_normal(key_values, -4.0, 4.0, full_shape, jnp.float32)
    ramp_x = 3.0 ** (0.5 * positions)
    log_half = 0.5 * math.log(10.0)
    row_scale = jnp.exp(jax.random.uniform(key_rows, (NY,), jnp.float32, -log_half, log_half))
    column_scale = jnp.exp(jax.random.uniform(key_columns, (NZ,), jnp.float32, -log_half, log_half))
    return values_raw * ramp_x[:, None, None] * row_scale[:, None] * column_scale


def draw_kspace(key, part):
    return scaled_field(jax.random.fold_in(key, 11), (COILS, 2))


def draw_prior_image(key, part):
    return scaled_field(jax.random.fold_in(key, 23), (2,))


def touch_ends(values, own_key, low, largest):
    dims = values.shape
    spot = [jax.random.randint(jax.random.fold_in(own_key, axis), (), 0, dims[axis]) for axis in range(len(dims))]
    values = values.at[tuple(spot)].set(low)
    longest = dims.index(max(dims))
    spot[longest] = (spot[longest] + 1) % dims[longest]
    return values.at[tuple(spot)].set(largest)


def steps_of(key, shape, cuts, smallest, high):
    level = 1.0
    for dim, shards_of in cuts:
        draws = jax.random.uniform(jax.random.fold_in(jax.random.fold_in(key, 6), dim), (shards_of,), jnp.float32, smallest / len(cuts), high / len(cuts))
        level = level * jnp.repeat(jnp.exp(draws), shape[dim] // shards_of).reshape((-1,) + (1,) * (len(shape) - 1 - dim))
    return level


def normal_values(rng, dims, spread, limit, cuts=(), kind=jnp.bfloat16):
    entries = jax.random.normal(rng, dims, jnp.float32) * spread
    if len(cuts) > 0:
        entries = steps_of(rng, dims, cuts, -0.22, 0.18) * entries
    return jnp.clip(entries, min=-limit, max=limit).astype(kind)


def setup_inputs(seed: int = 0) -> dict:
    key_of = jax.random.split(jax.random.key(seed), 8)
    return {
        "sensitivity": normal_values(key_of[0], (COILS, 2, NX, NY, NZ), ((2 * COILS) ** -0.5), 4.0, ((0, 4), (2, 8)), jnp.float32),
        "kspace": draw_kspace(jax.random.fold_in(key_of[7], 71), 0),
        "sampling": touch_ends((jax.random.randint(key_of[2], (NX, NY, NZ), 0, 3) < 1).astype(jnp.int32), jax.random.fold_in(key_of[2], 1), 0, 1),
        "prior_image": draw_prior_image(jax.random.fold_in(key_of[7], 71), 0),
        "w_first": normal_values(key_of[4], (CHANNELS, 2, 3, 3, 3), 54 ** -0.5, 0.875),
        "w_middle": normal_values(key_of[5], (LAYERS - 2, CHANNELS, CHANNELS, 3, 3, 3), (27 * CHANNELS) ** -0.5, 0.21875),
        "w_last": normal_values(key_of[6], (2, CHANNELS, 3, 3, 3), (27 * CHANNELS) ** -0.5, 0.21875),
    }


LAMBDA = 0.5


def to_kspace(field):
    values = jnp.fft.fft2(lax.complex(field[0], field[1]), axes=(-2, -1), norm="ortho")
    return jnp.stack([jnp.real(values), jnp.imag(values)])


def to_image(field):
    values = jnp.fft.ifft2(lax.complex(field[0], field[1]), axes=(-2, -1), norm="ortho")
    return jnp.stack([jnp.real(values), jnp.imag(values)])


def conj_apply(coil_maps, field):
    real_part = coil_maps[0] * field[0] + coil_maps[1] * field[1]
    imag_part = coil_maps[0] * field[1] - coil_maps[1] * field[0]
    return jnp.stack([real_part, imag_part])


def normal_image(direction, sensitivity, mask_f):
    def one_coil(total, coil_maps):
        coil_field = jnp.stack([coil_maps[0] * direction[0] - coil_maps[1] * direction[1],
                                coil_maps[0] * direction[1] + coil_maps[1] * direction[0]])
        spectrum = to_kspace(coil_field) * mask_f
        return total + conj_apply(coil_maps, to_image(spectrum)), None

    total, _ = lax.scan(one_coil, jnp.zeros_like(direction), sensitivity)
    return total


def adjoint_image(sensitivity, kspace, mask_f, template):
    def one_coil(total, pieces):
        coil_maps, measured = pieces
        return total + conj_apply(coil_maps, to_image(measured * mask_f)), None

    total, _ = lax.scan(one_coil, jnp.zeros_like(template), (sensitivity, kspace))
    return total


def conv_volume(activation, weight):
    result = lax.conv_general_dilated(activation[None].astype(jnp.float32), weight.astype(jnp.float32),
                                      (1, 1, 1), "SAME", dimension_numbers=("NCDHW", "OIDHW", "NCDHW"),
                                      precision=lax.Precision.HIGHEST)
    return result[0]


def reference(sensitivity, kspace, sampling, prior_image, w_first, w_middle, w_last):
    mask_f = sampling.astype(jnp.float32)
    rhs = adjoint_image(sensitivity, kspace, mask_f, prior_image) + LAMBDA * prior_image
    solution = jnp.zeros_like(prior_image)
    residual = rhs
    direction = rhs
    norm_now = jnp.sum(residual * residual)
    for step_index in range(ITERS):
        image_q = normal_image(direction, sensitivity, mask_f) + LAMBDA * direction
        step_size = norm_now / jnp.sum(direction * image_q)
        solution = solution + step_size * direction
        if step_index + 1 < ITERS:
            residual = residual - step_size * image_q
            norm_next = jnp.sum(residual * residual)
            direction = residual + (norm_next / norm_now) * direction
            norm_now = norm_next
    features = solution.astype(jnp.bfloat16)
    hidden = jax.nn.relu(conv_volume(features, w_first)).astype(jnp.bfloat16)
    for layer_index in range(w_middle.shape[0]):
        hidden = jax.nn.relu(conv_volume(hidden, w_middle[layer_index])).astype(jnp.bfloat16)
    correction = conv_volume(hidden, w_last)
    return solution, solution + correction
```

```python
import functools

import jax
import jax.numpy as jnp
import numpy as np
from jax import lax
from jax.experimental import pallas as pl
from jax.experimental.pallas import tpu as pltpu
from jax.sharding import PartitionSpec as P

LAMBDA = 0.5
MESH = pl.DeviceIdType.MESH


def dft_parts(length):
    positions = np.arange(length)
    angles = 2.0 * np.pi / length * (positions[:, None] * positions[None, :] % length)
    return np.cos(angles) / np.sqrt(length), np.sin(angles) / np.sqrt(length)


def halves(table):
    table = table.astype(np.float32)
    high = table.astype(jnp.bfloat16)
    low = (table - high.astype(np.float32)).astype(jnp.bfloat16)
    return high, low


def split(values):
    high = values.astype(jnp.bfloat16)
    return high, (values - high.astype(jnp.float32)).astype(jnp.bfloat16)


def multiply(left, right):
    return jnp.dot(left, right, preferred_element_type=jnp.float32)


def transform(real, imag, y_table, z_table):
    rows, width = real.shape
    high, low = split(jnp.concatenate([real, imag], axis=1))
    field = multiply(y_table[...], jnp.concatenate([high, low, high], axis=0))
    field = jnp.concatenate(
        [field[:rows, :width] + field[rows:, width:], field[:rows, width:] - field[rows:, :width]], axis=1
    )
    high, low = split(field)
    field = multiply(jnp.concatenate([high, low, high], axis=1), z_table[...])
    return field[:, :width], field[:, width:]


def total_of(values):
    return jnp.sum(jnp.sum(values, axis=0, keepdims=True), axis=1, keepdims=True)


BIAS = 128
LOW_HALF = 65535


def pack(real, imag):
    largest = jnp.maximum(
        jnp.max(jnp.abs(real), axis=0, keepdims=True), jnp.max(jnp.abs(imag), axis=0, keepdims=True)
    )
    exponent = jnp.maximum(jnp.ceil(jnp.log2(jnp.maximum(largest, 1e-35)) - 14.98), -110.0)
    scale = jnp.exp2(-exponent)
    real = jnp.round(real * scale).astype(jnp.int32)
    imag = jnp.round(imag * scale).astype(jnp.int32)
    code = exponent.astype(jnp.int32) + BIAS
    places = lax.broadcasted_iota(jnp.int32, (8, real.shape[1]), 0)
    bits = jnp.bitwise_and(jnp.right_shift(jnp.broadcast_to(code, places.shape), places), 1)
    head = jnp.bitwise_or(jnp.bitwise_and(real[:8], -2), bits)
    real = jnp.concatenate([head, real[8:]], axis=0)
    return jnp.bitwise_or(jnp.left_shift(real, 16), jnp.bitwise_and(imag, LOW_HALF))


def unpack(words):
    real = jnp.right_shift(words, 16)
    imag = jnp.right_shift(jnp.left_shift(words, 16), 16)
    places = lax.broadcasted_iota(jnp.int32, (8, words.shape[1]), 0)
    bits = jnp.left_shift(jnp.bitwise_and(real[:8], 1), places)
    code = jnp.sum(bits, axis=0, keepdims=True)
    scale = jnp.exp2((code - BIAS).astype(jnp.float32))
    return real.astype(jnp.float32) * scale, imag.astype(jnp.float32) * scale


def gradients_kernel(
    shares, coils, maps, measured, mask, prior, y_table, z_table,
    out, beside, part, outbox, inbox, own_rhs, rhs, own_residual, residual, note, notes, edges,
    block_send, block_recv, note_send, note_recv, edge_send, edge_recv,
):
    slab = lax.axis_index("slab")
    coil = lax.axis_index("coil")
    devices = shares * coils
    me = slab * coils + coil
    planes = maps.shape[1]
    block = prior.shape[2]
    tables = (y_table, z_table)

    def device_at(distance):
        other = lax.rem(me + distance, devices)
        return (other // coils, lax.rem(other, coils))

    barrier = pltpu.get_barrier_semaphore()
    for distance in range(1, devices):
        pl.semaphore_signal(barrier, inc=1, device_id=device_at(distance), device_id_type=MESH)

    def rows_of(index):
        return pl.ds(pl.multiple_of(index * block, block), block)

    mine = rows_of(coil)

    def scatter(phase, p):
        copies = []
        for distance in range(1, coils):
            target = lax.rem(coil + distance, coils)
            copies.append(
                pltpu.make_async_remote_copy(
                    src_ref=outbox.at[phase, p, rows_of(target)],
                    dst_ref=inbox.at[phase, distance - 1, p],
                    send_sem=block_send.at[phase, p, distance - 1],
                    recv_sem=block_recv.at[phase, p, distance - 1],
                    device_id=(slab, target),
                    device_id_type=MESH,
                )
            )
        for copy in copies:
            copy.start()
        return copies

    def gather_rhs(p):
        copies = []
        for distance in range(1, coils):
            copies.append(
                pltpu.make_async_remote_copy(
                    src_ref=outbox.at[2, p, pl.ds(0, block)],
                    dst_ref=inbox.at[2, distance - 1, p],
                    send_sem=block_send.at[2, p, distance - 1],
                    recv_sem=block_recv.at[2, p, distance - 1],
                    device_id=(slab, lax.rem(coil + distance, coils)),
                    device_id_type=MESH,
                )
            )
        for copy in copies:
            copy.start()
        return copies

    def gather(p):
        copies = []
        for distance in range(1, coils):
            copies.append(
                pltpu.make_async_remote_copy(
                    src_ref=residual.at[:, p, mine],
                    dst_ref=residual.at[:, p, mine],
                    send_sem=block_send.at[3, p, distance - 1],
                    recv_sem=block_recv.at[3, p, distance - 1],
                    device_id=(slab, lax.rem(coil + distance, coils)),
                    device_id_type=MESH,
                )
            )
        for copy in copies:
            copy.start()
        return copies

    def tell(phase):
        copies = []
        for distance in range(1, devices):
            copies.append(
                pltpu.make_async_remote_copy(
                    src_ref=note.at[phase],
                    dst_ref=notes.at[phase, distance - 1],
                    send_sem=note_send.at[phase, distance - 1],
                    recv_sem=note_recv.at[phase, distance - 1],
                    device_id=device_at(distance),
                    device_id_type=MESH,
                )
            )
        for copy in copies:
            copy.start()
        return copies

    margin = edges.shape[4]
    above = lax.rem(coil + coils - 1, coils)
    below = lax.rem(coil + 1, coils)

    def send_edges(source, which, p):
        copies = []
        for side, first, target in ((0, block - margin, below), (1, 0, above)):
            copies.append(
                pltpu.make_async_remote_copy(
                    src_ref=source.at[:, p, first : first + margin],
                    dst_ref=edges.at[which, side, :, p],
                    send_sem=edge_send.at[which, side, p],
                    recv_sem=edge_recv.at[which, side, p],
                    device_id=(slab, target),
                    device_id_type=MESH,
                )
            )
        for copy in copies:
            copy.start()
        return copies

    def finish(copies):
        for copy in copies:
            copy.wait()

    lanes = lax.broadcasted_iota(jnp.int32, (1, note.shape[2]), 1)

    def write_note(phase, values):
        line = jnp.zeros(lanes.shape, jnp.float32)
        for index, value in enumerate(values):
            line = jnp.where(lanes == index, value, line)
        note[phase] = line

    def read_notes(phase, count):
        line = note[phase]
        for distance in range(1, devices):
            line = line + notes[phase, distance - 1]
        return [jnp.sum(jnp.where(lanes == index, line, 0.0), axis=1, keepdims=True) for index in range(count)]

    def backward_part(real, imag, phase, p):
        imag, real = transform(imag, real, *tables)
        part_re = maps[0, p] * real + maps[1, p] * imag
        part_im = maps[0, p] * imag - maps[1, p] * real
        part[phase, 0, p] = part_re
        part[phase, 1, p] = part_im
        for index in range(coils):
            span = slice(index * block, (index + 1) * block)
            outbox[phase, p, span] = pack(part_re[span], part_im[span])

    def forward(image_re, image_im, p):
        real = maps[0, p] * image_re - maps[1, p] * image_im
        imag = maps[0, p] * image_im + maps[1, p] * image_re
        real, imag = transform(real, imag, *tables)
        sampled = mask[p].astype(jnp.float32)
        return real * sampled, imag * sampled

    def reduced(phase, p):
        real = part[phase, 0, p, mine]
        imag = part[phase, 1, p, mine]
        for distance in range(1, coils):
            more = unpack(inbox[phase, distance - 1, p])
            real = real + more[0]
            imag = imag + more[1]
        return real, imag

    for p in range(planes):
        sampled = mask[p].astype(jnp.float32)
        backward_part(measured[0, p] * sampled, measured[1, p] * sampled, 0, p)
    pl.semaphore_wait(barrier, devices - 1)
    pending = [scatter(0, p) for p in range(planes)]
    gathers = []
    norm = jnp.zeros((1, 1), jnp.float32)
    edge_copies = []
    for p in range(planes):
        finish(pending[p])
        real, imag = reduced(0, p)
        real = real + LAMBDA * prior[0, p]
        imag = imag + LAMBDA * prior[1, p]
        outbox[2, p, :block] = pack(real, imag)
        gathers.append(gather_rhs(p))
        own_rhs[0, p] = real
        own_rhs[1, p] = imag
        rhs[0, p, mine] = real
        rhs[1, p, mine] = imag
        norm = norm + total_of(real * real) + total_of(imag * imag)
    for p in range(planes):
        edge_copies.extend(send_edges(own_rhs, 0, p))
    energy = LAMBDA * norm
    pending = []
    for p in range(planes):
        finish(gathers[p])
        for distance in range(1, coils):
            source = rows_of(lax.rem(coil + coils - distance, coils))
            real, imag = unpack(inbox[2, distance - 1, p])
            rhs[0, p, source] = real
            rhs[1, p, source] = imag
        real, imag = forward(rhs[0, p], rhs[1, p], p)
        energy = energy + total_of(real * real) + total_of(imag * imag)
        if p == planes - 1:
            write_note(0, [norm, energy])
            first_notes = tell(0)
        backward_part(real, imag, 1, p)
        pending.append(scatter(1, p))
    finish(first_notes)
    norm, curvature = read_notes(0, 2)
    step = norm / curvature
    gathers = []
    norm_next = jnp.zeros((1, 1), jnp.float32)
    cross = jnp.zeros((1, 1), jnp.float32)
    for p in range(planes):
        finish(pending[p])
        images = reduced(1, p)
        for h in range(2):
            direction = own_rhs[h, p]
            image = images[h] + LAMBDA * direction
            value = direction - step * image
            own_residual[h, p] = value
            residual[h, p, mine] = value.astype(jnp.bfloat16)
        gathers.append(gather(p))
        for h in range(2):
            value = own_residual[h, p]
            image = images[h] + LAMBDA * own_rhs[h, p]
            norm_next = norm_next + total_of(value * value)
            cross = cross + total_of(value * image)
    for p in range(planes):
        edge_copies.extend(send_edges(own_residual, 1, p))
    energy = LAMBDA * norm_next
    for p in range(planes):
        finish(gathers[p])
        real, imag = forward(residual[0, p].astype(jnp.float32), residual[1, p].astype(jnp.float32), p)
        energy = energy + total_of(real * real) + total_of(imag * imag)
    write_note(1, [norm_next, energy, cross])
    finish(tell(1))
    norm_next, energy, cross = read_notes(1, 3)
    ratio = norm_next / norm
    curvature = energy + 2.0 * ratio * cross + ratio * ratio * curvature
    step_next = norm_next / curvature
    finish(edge_copies)
    for h in range(2):
        for p in range(planes):
            direction = own_rhs[h, p]
            out[h, p] = step * direction + step_next * (own_residual[h, p] + ratio * direction)
            for side, inside in ((0, coil > 0), (1, coil < coils - 1)):
                direction = edges[0, side, h, p]
                value = step * direction + step_next * (edges[1, side, h, p] + ratio * direction)
                beside[side, h, p] = jnp.where(inside, value, 0.0)


def gradients(maps, measured, mask, prior, margin):
    planes, rows, width = mask.shape
    block = prior.shape[2]
    shares = lax.axis_size("slab")
    coils = lax.axis_size("coil")
    cosine, sine = dft_parts(rows)
    high, low = halves(np.concatenate([cosine, sine]))
    y_table = np.concatenate([high, high, low], axis=1)
    cosine, sine = dft_parts(width)
    high, low = halves(np.block([[cosine, -sine], [sine, cosine]]))
    z_table = np.concatenate([high, high, low], axis=0)
    image = (2, planes, rows, width)
    brick = (2, planes, block, width)
    margins = (2, 2, planes, margin, width)
    return pl.pallas_call(
        functools.partial(gradients_kernel, shares, coils),
        out_shape=[jax.ShapeDtypeStruct(dims, jnp.float32) for dims in (brick, margins)],
        in_specs=[pl.BlockSpec(memory_space=pltpu.VMEM)] * 6,
        out_specs=[pl.BlockSpec(memory_space=pltpu.VMEM)] * 2,
        scratch_shapes=[
            pltpu.VMEM((2,) + image, jnp.float32),
            pltpu.VMEM((3, planes, rows, width), jnp.int32),
            pltpu.VMEM((3, coils - 1, planes, block, width), jnp.int32),
            pltpu.VMEM(brick, jnp.float32),
            pltpu.VMEM(image, jnp.float32),
            pltpu.VMEM(brick, jnp.float32),
            pltpu.VMEM(image, jnp.bfloat16),
            pltpu.VMEM((2, 1, 128), jnp.float32),
            pltpu.VMEM((2, shares * coils - 1, 1, 128), jnp.float32),
            pltpu.VMEM((2,) + margins, jnp.float32),
            pltpu.SemaphoreType.DMA((4, planes, coils - 1)),
            pltpu.SemaphoreType.DMA((4, planes, coils - 1)),
            pltpu.SemaphoreType.DMA((2, shares * coils - 1)),
            pltpu.SemaphoreType.DMA((2, shares * coils - 1)),
            pltpu.SemaphoreType.DMA((2, 2, planes)),
            pltpu.SemaphoreType.DMA((2, 2, planes)),
        ],
        compiler_params=pltpu.CompilerParams(
            collective_id=0, has_side_effects=True, vmem_limit_bytes=56 * 1024 * 1024
        ),
    )(maps, measured, mask, prior, y_table, z_table)


def block_weights(weight, x_outs, y_outs, in_pad, out_pad):
    weight = jnp.pad(weight, ((0, out_pad), (0, in_pad), (0, 0), (0, 0), (0, 0)))
    weight = jnp.transpose(weight, (4, 0, 3, 2, 1))
    parts = []
    for x_out in range(x_outs):
        for y_out in range(y_outs):
            spread = ((0, 0), (0, 0), (y_out, y_outs - 1 - y_out), (x_out, x_outs - 1 - x_out), (0, 0))
            parts.append(jnp.pad(weight, spread))
    stacked = jnp.stack(parts)
    return stacked.reshape(stacked.shape[0] * stacked.shape[1] * stacked.shape[2], -1)


def conv_rows(weight_ref, source, sink, rows, planes, x_outs, y_outs, group, top, height, last):
    width = source.shape[-1]
    channels = source.shape[2]
    weight_rows = weight_ref.shape[0]
    outs = weight_rows // (3 * x_outs * y_outs)
    lanes = lax.broadcasted_iota(jnp.int32, (outs, width), 1)
    depth = (y_outs + 2) * (x_outs + 2) * channels

    def step(index, carry):
        y = index * y_outs
        for first in range(0, planes, x_outs * group):
            blocks = [
                source[pl.ds(y, y_outs + 2), first + k * x_outs : first + (k + 1) * x_outs + 2].reshape(depth, width)
                for k in range(group)
            ]
            taken = jnp.concatenate(blocks, axis=1) if group > 1 else blocks[0]
            product = jnp.dot(weight_ref[...], taken, preferred_element_type=jnp.float32)
            for x_out in range(x_outs):
                for y_out in range(y_outs):
                    base = (x_out * y_outs + y_out) * 3 * outs
                    y_now = y + y_out
                    inside = jnp.logical_and(top + y_now >= 0, top + y_now < height)
                    for k in range(group):
                        span = slice(k * width, (k + 1) * width)
                        before = product[base : base + outs, span]
                        centre = product[base + outs : base + 2 * outs, span]
                        after = product[base + 2 * outs : base + 3 * outs, span]
                        before = jnp.where(lanes == 0, 0.0, pltpu.roll(before, 1, 1))
                        after = jnp.where(lanes == width - 1, 0.0, pltpu.roll(after, width - 1, 1))
                        value = centre + before + after
                        plane = first + k * x_outs + x_out
                        if last:
                            sink[y_now, plane] = value
                        else:
                            value = jnp.where(inside, jnp.maximum(value, 0.0), 0.0)
                            sink[y_now, plane + 1] = value.astype(jnp.bfloat16)
        return carry

    lax.fori_loop(0, rows // y_outs, step, 0)


def spread_weights(taps, wide, x_outs, y_outs):
    count, channels = taps.shape[2:]
    span = (x_outs + 2) * channels
    empty = jnp.zeros((count, channels), taps.dtype)
    for x_out in range(x_outs):
        for y_out in range(y_outs):
            base = (x_out * y_outs + y_out) * count
            for y_in in range(y_outs + 2):
                tap = y_in - y_out
                if 0 <= tap < 3:
                    shifts = [x_in - x_out for x_in in range(x_outs + 2)]
                    pieces = [taps[u, tap] if 0 <= u < 3 else empty for u in shifts]
                    block = jnp.concatenate(pieces, axis=1)
                else:
                    block = jnp.zeros((count, span), taps.dtype)
                wide[base : base + count, y_in * span : (y_in + 1) * span] = block


def denoise_kernel(
    x_outs, y_outs, group, rows, block_rows, height, features, first, middle, final, out, even, odd, wide
):
    planes = features.shape[1] - 2
    layers = middle.shape[0] + 2
    top = lax.axis_index("coil") * block_rows + lax.axis_index("slab") * rows
    buffers = (even, odd)
    for buffer in buffers:
        edge = jnp.zeros((buffer.shape[0],) + buffer.shape[2:], buffer.dtype)
        buffer[:, 0] = edge
        buffer[:, planes + 1] = edge
    shared = (planes, x_outs, y_outs, group)
    left = layers - 1
    for layer in range(layers - 2):
        spread_weights(middle.at[layer], wide.at[layer], x_outs, y_outs)
    conv_rows(first, features, even, rows + 2 * left, *shared, top - left, height, False)
    for layer in range(layers - 2):
        left = left - 1
        conv_rows(
            wide.at[layer], buffers[layer % 2], buffers[(layer + 1) % 2],
            rows + 2 * left, *shared, top - left, height, False,
        )
    conv_rows(final, buffers[(layers - 2) % 2], out, rows, *shared, top, height, True)


def denoise(features, w_first, w_middle, w_last, rows, block_rows, height):
    planes = features.shape[1]
    width = features.shape[3]
    channels = w_first.shape[0]
    layers = w_middle.shape[0] + 2
    x_outs = 2 if planes % 2 == 0 else 1
    y_outs = 2 if rows % 2 == 0 else 1
    group = 2 if (planes // x_outs) % 2 == 0 else 1
    in_rows = 16
    features = jnp.pad(features, ((0, 0), (1, 1), (0, in_rows - features.shape[2]), (0, 0)))
    first = block_weights(w_first, x_outs, y_outs, in_rows - w_first.shape[1], 0)
    middle = jnp.transpose(w_middle, (0, 3, 4, 5, 1, 2)).reshape(layers - 2, 3, 3, 3 * channels, channels)
    wide = (layers - 2, x_outs * y_outs * 3 * channels, (x_outs + 2) * (y_outs + 2) * channels)
    final = block_weights(w_last, x_outs, y_outs, 0, -w_last.shape[0] % 8)
    outs = w_last.shape[0]
    held = (rows + 2 * (layers - 1), planes + 2, channels, width)
    result = pl.pallas_call(
        functools.partial(denoise_kernel, x_outs, y_outs, group, rows, block_rows, height),
        out_shape=jax.ShapeDtypeStruct((rows, planes, outs + -outs % 8, width), jnp.float32),
        in_specs=[pl.BlockSpec(memory_space=pltpu.VMEM)] * 4,
        out_specs=pl.BlockSpec(memory_space=pltpu.VMEM),
        scratch_shapes=[pltpu.VMEM(dims, jnp.bfloat16) for dims in (held, held, wide)],
        compiler_params=pltpu.CompilerParams(vmem_limit_bytes=48 * 1024 * 1024),
    )(features, first, middle, final)
    return result[:, :, :outs]


def body(sensitivity, kspace, sampling, prior_image, w_first, w_middle, w_last):
    halo = w_middle.shape[0] + 2
    margin = halo + -halo % 8
    brick, beside = gradients(sensitivity[0], kspace[0], sampling, prior_image, margin)
    len_y = sampling.shape[1]
    block_rows = prior_image.shape[2]
    shares = lax.axis_size("slab")
    rows = block_rows // shares
    mine = jnp.concatenate([beside[0, :, :, margin - halo :], brick, beside[1, :, :, :halo]], axis=2)
    mine = mine.astype(jnp.bfloat16)
    mine = jnp.transpose(mine, (2, 1, 0, 3))
    pieces = jnp.stack([mine[s * rows : (s + 1) * rows + 2 * halo] for s in range(shares)])
    taken = lax.all_to_all(pieces, "slab", 0, 0)
    features = jnp.moveaxis(taken, 0, 1).reshape((rows + 2 * halo, -1) + taken.shape[3:])
    correction = denoise(features, w_first, w_middle, w_last, rows, block_rows, len_y)
    local = prior_image.shape[1]
    pieces = jnp.moveaxis(correction.reshape((rows, shares, local) + correction.shape[2:]), 1, 0)
    taken = lax.all_to_all(pieces, "slab", 0, 0)
    correction = jnp.transpose(taken.reshape((block_rows,) + taken.shape[2:]), (2, 1, 0, 3))
    return (brick, brick + correction)


def solution(mesh):
    placed = (
        P("coil", None, "slab", None, None),
        P("coil", None, "slab", None, None),
        P("slab", None, None),
        P(None, "slab", "coil", None),
        P(),
        P(),
        P(),
    )
    return jax.shard_map(
        body,
        mesh=mesh,
        in_specs=placed,
        out_specs=(P(None, "slab", "coil", None), P(None, "slab", "coil", None)),
        check_vma=False,
    )
```

```python
import functools

import jax
import jax.numpy as jnp
import numpy as np
from jax import lax
from jax.experimental import pallas as pl
from jax.experimental.pallas import tpu as pltpu
from jax.sharding import PartitionSpec as P

LAMBDA = 0.5
MESH = pl.DeviceIdType.MESH


def dft_parts(length):
    positions = np.arange(length)
    angles = 2.0 * np.pi / length * (positions[:, None] * positions[None, :] % length)
    return np.cos(angles) / np.sqrt(length), np.sin(angles) / np.sqrt(length)


def halves(table):
    table = table.astype(np.float32)
    high = table.astype(jnp.bfloat16)
    low = (table - high.astype(np.float32)).astype(jnp.bfloat16)
    return high, low


def split(values):
    high = values.astype(jnp.bfloat16)
    return high, (values - high.astype(jnp.float32)).astype(jnp.bfloat16)


def multiply(left, right):
    return jnp.dot(left, right, preferred_element_type=jnp.float32)


def transform(real, imag, y_table, z_table):
    rows, width = real.shape
    high, low = split(jnp.concatenate([real, imag], axis=1))
    field = multiply(y_table[...], jnp.concatenate([high, low, high], axis=0))
    field = jnp.concatenate(
        [field[:rows, :width] + field[rows:, width:], field[:rows, width:] - field[rows:, :width]], axis=1
    )
    high, low = split(field)
    field = multiply(jnp.concatenate([high, low, high], axis=1), z_table[...])
    return field[:, :width], field[:, width:]


def total_of(values):
    return jnp.sum(jnp.sum(values, axis=0, keepdims=True), axis=1, keepdims=True)


BIAS = 128
LOW_HALF = 65535


def pack(real, imag):
    largest = jnp.maximum(
        jnp.max(jnp.abs(real), axis=0, keepdims=True), jnp.max(jnp.abs(imag), axis=0, keepdims=True)
    )
    exponent = jnp.maximum(jnp.ceil(jnp.log2(jnp.maximum(largest, 1e-35)) - 14.98), -110.0)
    scale = jnp.exp2(-exponent)
    real = jnp.round(real * scale).astype(jnp.int32)
    imag = jnp.round(imag * scale).astype(jnp.int32)
    code = exponent.astype(jnp.int32) + BIAS
    places = lax.broadcasted_iota(jnp.int32, (8, real.shape[1]), 0)
    bits = jnp.bitwise_and(jnp.right_shift(jnp.broadcast_to(code, places.shape), places), 1)
    head = jnp.bitwise_or(jnp.bitwise_and(real[:8], -2), bits)
    real = jnp.concatenate([head, real[8:]], axis=0)
    return jnp.bitwise_or(jnp.left_shift(real, 16), jnp.bitwise_and(imag, LOW_HALF))


def unpack(words):
    real = jnp.right_shift(words, 16)
    imag = jnp.right_shift(jnp.left_shift(words, 16), 16)
    places = lax.broadcasted_iota(jnp.int32, (8, words.shape[1]), 0)
    bits = jnp.left_shift(jnp.bitwise_and(real[:8], 1), places)
    code = jnp.sum(bits, axis=0, keepdims=True)
    scale = jnp.exp2((code - BIAS).astype(jnp.float32))
    return real.astype(jnp.float32) * scale, imag.astype(jnp.float32) * scale


def spread(blocks, x_out):
    empty = jnp.zeros_like(blocks[0])
    return jnp.concatenate([empty] * x_out + blocks + [empty] * (1 - x_out), axis=1)


def first_weights(taps, base, table):
    outs = taps.shape[-1]
    for u in range(3):
        for v in range(3):
            for t in range(3):
                index = ((v * 3 + t) * 3 + u) * 2
                base[index : index + 2, :outs] = taps[u, v, t].astype(jnp.float32)
    window = (24, table.shape[0])
    row = lax.broadcasted_iota(jnp.int32, window, 0)
    place = row - 2 * (lax.broadcasted_iota(jnp.int32, window, 1) // outs) - 2
    rest = jnp.zeros((8, window[1]), jnp.float32)
    blocks = []
    for v in range(3):
        for t in range(3):
            block = jnp.zeros(window, jnp.float32)
            for k in range(6):
                index = (v * 3 + t) * 6 + k
                line = jnp.concatenate([base[index : index + 1, :outs]] * (window[1] // outs), axis=1)
                block = jnp.where(place == k, line, block)
            blocks.append(block)
        blocks.append(rest)
    blocks.append(jnp.zeros((16, window[1]), jnp.float32))
    table[...] = jnp.transpose(jnp.concatenate(blocks, axis=0)).astype(table.dtype)


def middle_weights(taps, table, y_outs):
    count, channels = taps.shape[3:]
    span = 4 * channels
    table[...] = jnp.zeros(table.shape, table.dtype)
    for layer in range(taps.shape[0]):
        for v in range(3):
            for x_out in range(2):
                block = spread([taps[layer, u, v] for u in range(3)], x_out)
                for y_out in range(y_outs):
                    base = (x_out * y_outs + y_out) * count
                    y_in = y_out + v
                    table[layer, base : base + count, y_in * span : (y_in + 1) * span] = block


def last_weights(taps, table, tall):
    channels = taps.shape[-1]
    span = 4 * channels
    row = lax.broadcasted_iota(jnp.int32, (tall, span), 0)
    for t in range(3):
        for x_out in range(2):
            lines = [spread([taps[u, v, t].astype(jnp.float32) for u in range(3)], x_out) for v in range(3)]
            for o in range(2):
                base = ((t * 2 + x_out) * 2 + o) * tall
                for y_in in range(table.shape[1] // span):
                    block = jnp.zeros((tall, span), jnp.float32)
                    for v in range(3):
                        block = jnp.where(row == y_in - v, lines[v][o : o + 1], block)
                    table[base : base + tall, y_in * span : (y_in + 1) * span] = block.astype(table.dtype)


def along_z(before, centre, after, lanes):
    width = centre.shape[1]
    before = jnp.where(lanes == 0, 0.0, pltpu.roll(before, 1, 1))
    after = jnp.where(lanes == width - 1, 0.0, pltpu.roll(after, width - 1, 1))
    return centre + before + after


def conv_first(table, taken, sink, rows, top, height):
    outs = sink.shape[2]
    width = sink.shape[3]
    depth = 3 * taken.shape[1]
    for y in range(rows):
        inside = jnp.logical_and(top + y >= 0, top + y < height)
        product = multiply(table[:, :depth], taken[y : y + 3].reshape(depth, taken.shape[2]))
        for group in range(taken.shape[2] // width):
            for q in range(table.shape[0] // outs):
                value = product[q * outs : (q + 1) * outs, group * width : (group + 1) * width]
                value = jnp.where(inside, jnp.maximum(value, 0.0), 0.0)
                sink[y, group * (table.shape[0] // outs) + q + 1] = value.astype(jnp.bfloat16)


def conv_middle(table, source, sink, rows, y_outs, top, height):
    planes, outs, width = source.shape[1] - 2, source.shape[2], source.shape[3]
    lanes = lax.broadcasted_iota(jnp.int32, (outs, width), 1)
    depth = (y_outs + 2) * 4 * outs
    group = 2 if planes % 4 == 0 else 1
    for y in range(0, rows, y_outs):
        for first in range(0, planes, 2 * group):
            taken = [
                source[y : y + y_outs + 2, first + 2 * k : first + 2 * k + 4].reshape(depth, width)
                for k in range(group)
            ]
            product = multiply(table[...], jnp.concatenate(taken, axis=1))
            for x_out in range(2):
                for y_out in range(y_outs):
                    base = (x_out * y_outs + y_out) * 3 * outs
                    inside = jnp.logical_and(top + y + y_out >= 0, top + y + y_out < height)
                    for k in range(group):
                        parts = [
                            product[base + t * outs : base + (t + 1) * outs, k * width : (k + 1) * width]
                            for t in range(3)
                        ]
                        value = along_z(*parts, lanes)
                        value = jnp.where(inside, jnp.maximum(value, 0.0), 0.0)
                        sink[y + y_out, first + 2 * k + x_out + 1] = value.astype(jnp.bfloat16)


def conv_last(table, source, sink, rows):
    planes, channels, width = source.shape[1] - 2, source.shape[2], source.shape[3]
    tall = table.shape[0] // 3
    lanes = lax.broadcasted_iota(jnp.int32, (tall, width), 1)
    depth = (rows + 2) * 4 * channels
    group = 2 if planes % 4 == 0 else 1
    for first in range(0, planes, 2 * group):
        taken = [
            source[: rows + 2, first + 2 * k : first + 2 * k + 4].reshape(depth, width) for k in range(group)
        ]
        product = multiply(table[...], jnp.concatenate(taken, axis=1))
        for k in range(group):
            parts = [product[t * tall : (t + 1) * tall, k * width : (k + 1) * width] for t in range(3)]
            sink[first // 2 + k] = along_z(*parts, lanes).reshape(sink.shape[1:])


def step_kernel(
    shares, coils, maps, measured, mask, prior, y_table, z_table, w_first, w_middle, w_last,
    out, refined,
    part, outbox, inbox, own_rhs, rhs, own_residual, residual, note, notes, fields, taken_fields,
    base, first_table, middle_table, last_table, shifted, even, odd, corrections, arrived,
    block_send, block_recv, note_send, note_recv, edge_send, edge_recv, field_send, field_recv, back_send, back_recv,
):
    slab = lax.axis_index("slab")
    coil = lax.axis_index("coil")
    devices = shares * coils
    me = slab * coils + coil
    planes = maps.shape[1]
    height, width = maps.shape[2:]
    block = prior.shape[2]
    rows = block // shares
    layers = w_middle.shape[0] + 2
    halo = layers
    y_outs = 2 if rows % 2 == 0 else 1
    tables = (y_table, z_table)

    def device_at(distance):
        other = lax.rem(me + distance, devices)
        return (other // coils, lax.rem(other, coils))

    barrier = pltpu.get_barrier_semaphore()
    for distance in range(1, devices):
        pl.semaphore_signal(barrier, inc=1, device_id=device_at(distance), device_id_type=MESH)

    def rows_of(index):
        return pl.ds(pl.multiple_of(index * block, block), block)

    mine = rows_of(coil)

    def send(source, target, send_sem, recv_sem, device):
        copy = pltpu.make_async_remote_copy(
            src_ref=source, dst_ref=target, send_sem=send_sem, recv_sem=recv_sem,
            device_id=device, device_id_type=MESH,
        )
        copy.start()
        return copy

    def to_coils(phase, p, source, target):
        copies = []
        for distance in range(1, coils):
            other = lax.rem(coil + distance, coils)
            copies.append(
                send(
                    source(other), target(distance), block_send.at[phase, p, distance - 1],
                    block_recv.at[phase, p, distance - 1], (slab, other),
                )
            )
        return copies

    def scatter(phase, p):
        return to_coils(
            phase, p, lambda other: outbox.at[phase, p, rows_of(other)],
            lambda distance: inbox.at[phase, distance - 1, p],
        )

    def gather_rhs(p):
        return to_coils(
            2, p, lambda other: outbox.at[2, p, pl.ds(0, block)], lambda distance: inbox.at[2, distance - 1, p]
        )

    def gather(p):
        return to_coils(
            3, p, lambda other: residual.at[:, p, mine], lambda distance: residual.at[:, p, mine]
        )

    def tell(phase):
        copies = []
        for distance in range(1, devices):
            copies.append(
                send(
                    note.at[phase], notes.at[phase, distance - 1], note_send.at[phase, distance - 1],
                    note_recv.at[phase, distance - 1], device_at(distance),
                )
            )
        return copies

    def send_edges(which):
        above = lax.rem(coil + coils - 1, coils)
        below = lax.rem(coil + 1, coils)
        ends = ((block, 0, below), (halo, halo + block, above))
        return [
            send(
                fields.at[which, pl.ds(source, halo)], fields.at[which, pl.ds(target, halo)],
                edge_send.at[which, side], edge_recv.at[which, side], (slab, other),
            )
            for side, (source, target, other) in enumerate(ends)
        ]

    deep = rows + 2 * halo

    def send_fields(which, copies):
        finish(copies)
        top_edge = fields[which, :halo]
        fields[which, :halo] = jnp.where(coil > 0, top_edge, 0.0)
        low_edge = fields[which, halo + block :]
        fields[which, halo + block :] = jnp.where(coil < coils - 1, low_edge, 0.0)
        copies = []
        for distance in range(1, shares):
            other = lax.rem(slab + distance, shares)
            copies.append(
                send(
                    fields.at[which, pl.ds(other * rows, deep)], taken_fields.at[which, :, slab + 1],
                    field_send.at[which, distance - 1], field_recv.at[which, distance - 1], (other, coil),
                )
            )
        taken_fields[which, :, slab + 1] = fields[which, pl.ds(slab * rows, deep)]
        return copies

    def finish(copies):
        for copy in copies:
            copy.wait()

    lanes = lax.broadcasted_iota(jnp.int32, (1, note.shape[2]), 1)

    def write_note(phase, values):
        line = jnp.zeros(lanes.shape, jnp.float32)
        for index, value in enumerate(values):
            line = jnp.where(lanes == index, value, line)
        note[phase] = line

    def read_notes(phase, count):
        line = note[phase]
        for distance in range(1, devices):
            line = line + notes[phase, distance - 1]
        return [jnp.sum(jnp.where(lanes == index, line, 0.0), axis=1, keepdims=True) for index in range(count)]

    def backward_part(real, imag, phase, p):
        imag, real = transform(imag, real, *tables)
        part_re = maps[0, p] * real + maps[1, p] * imag
        part_im = maps[0, p] * imag - maps[1, p] * real
        part[phase, 0, p] = part_re
        part[phase, 1, p] = part_im
        for index in range(coils):
            span = slice(index * block, (index + 1) * block)
            outbox[phase, p, span] = pack(part_re[span], part_im[span])

    def forward(image_re, image_im, p):
        real = maps[0, p] * image_re - maps[1, p] * image_im
        imag = maps[0, p] * image_im + maps[1, p] * image_re
        real, imag = transform(real, imag, *tables)
        sampled = mask[p].astype(jnp.float32)
        return real * sampled, imag * sampled

    def reduced(phase, p):
        real = part[phase, 0, p, mine]
        imag = part[phase, 1, p, mine]
        for distance in range(1, coils):
            more = unpack(inbox[phase, distance - 1, p])
            real = real + more[0]
            imag = imag + more[1]
        return real, imag

    pending = []
    for p in range(planes):
        sampled = mask[p].astype(jnp.float32)
        backward_part(measured[0, p] * sampled, measured[1, p] * sampled, 0, p)
        if p == 0:
            pl.semaphore_wait(barrier, devices - 1)
        pending.append(scatter(0, p))
    first_weights(w_first, base, first_table)
    last_weights(w_last, last_table, last_table.shape[0] // 12)
    total = taken_fields.shape[2]
    for which in range(2):
        for outer in (0, total - 1):
            taken_fields[which, :, outer] = jnp.zeros((deep,) + taken_fields.shape[3:], jnp.float32)
    shifted[...] = jnp.zeros(shifted.shape, shifted.dtype)
    for buffer in (even, odd):
        for outer in (0, buffer.shape[1] - 1):
            buffer[:, outer] = jnp.zeros((buffer.shape[0],) + buffer.shape[2:], buffer.dtype)
    gathers = []
    norm = jnp.zeros((1, 1), jnp.float32)
    for p in range(planes):
        finish(pending[p])
        real, imag = reduced(0, p)
        real = real + LAMBDA * prior[0, p]
        imag = imag + LAMBDA * prior[1, p]
        outbox[2, p, :block] = pack(real, imag)
        gathers.append(gather_rhs(p))
        for h, value in enumerate((real, imag)):
            own_rhs[h, p] = value
            rhs[h, p, mine] = value
            fields[0, halo : halo + block, 2 * p + h] = value
            norm = norm + total_of(value * value)
    edge_copies = send_edges(0)
    middle_weights(w_middle, middle_table, y_outs)
    energy = LAMBDA * norm
    pending = []
    for p in range(planes):
        finish(gathers[p])
        for distance in range(1, coils):
            source = rows_of(lax.rem(coil + coils - distance, coils))
            real, imag = unpack(inbox[2, distance - 1, p])
            rhs[0, p, source] = real
            rhs[1, p, source] = imag
        real, imag = forward(rhs[0, p], rhs[1, p], p)
        energy = energy + total_of(real * real) + total_of(imag * imag)
        if p == planes - 1:
            write_note(0, [norm, energy])
            first_notes = tell(0)
        backward_part(real, imag, 1, p)
        pending.append(scatter(1, p))
    field_copies = send_fields(0, edge_copies)
    finish(first_notes)
    norm, curvature = read_notes(0, 2)
    step = norm / curvature
    gathers = []
    norm_next = jnp.zeros((1, 1), jnp.float32)
    cross = jnp.zeros((1, 1), jnp.float32)
    for p in range(planes):
        finish(pending[p])
        images = reduced(1, p)
        for h in range(2):
            direction = own_rhs[h, p]
            image = images[h] + LAMBDA * direction
            value = direction - step * image
            own_residual[h, p] = value
            residual[h, p, mine] = value.astype(jnp.bfloat16)
            fields[1, halo : halo + block, 2 * p + h] = value
        gathers.append(gather(p))
        for h in range(2):
            value = own_residual[h, p]
            image = images[h] + LAMBDA * own_rhs[h, p]
            norm_next = norm_next + total_of(value * value)
            cross = cross + total_of(value * image)
    edge_copies = send_edges(1)
    energy = LAMBDA * norm_next
    for p in range(planes):
        finish(gathers[p])
        if p == planes - 1:
            field_copies = field_copies + send_fields(1, edge_copies)
        real, imag = forward(residual[0, p].astype(jnp.float32), residual[1, p].astype(jnp.float32), p)
        energy = energy + total_of(real * real) + total_of(imag * imag)
    write_note(1, [norm_next, energy, cross])
    last_notes = tell(1)
    finish(field_copies)
    finish(last_notes)
    norm_next, energy, cross = read_notes(1, 3)
    ratio = norm_next / norm
    curvature = energy + 2.0 * ratio * cross + ratio * ratio * curvature
    step_next = norm_next / curvature
    share = step + step_next * ratio
    across = lax.broadcasted_iota(jnp.int32, (4 * total, width), 1)
    for y in range(deep):
        line = share * taken_fields[0, y].reshape(4 * total, width)
        line = line + step_next * taken_fields[1, y].reshape(4 * total, width)
        line = line.astype(jnp.bfloat16).astype(jnp.float32)
        before = jnp.where(across == 0, 0.0, pltpu.roll(line, 1, 1))
        after = jnp.where(across == width - 1, 0.0, pltpu.roll(line, width - 1, 1))
        for group in range(shifted.shape[2] // width):
            span = slice(16 * group, 16 * group + 24)
            piece = jnp.concatenate([before[span], line[span], after[span], jnp.zeros((8, width), jnp.float32)], axis=0)
            shifted[y, :, group * width : (group + 1) * width] = piece.astype(jnp.bfloat16)
    for h in range(2):
        for p in range(planes):
            out[h, p] = share * own_rhs[h, p] + step_next * own_residual[h, p]
    top = coil * block + slab * rows
    left = layers - 1
    conv_first(first_table, shifted, even, rows + 2 * left, top - left, height)
    buffers = (even, odd)
    for layer in range(layers - 2):
        left = left - 1
        conv_middle(
            middle_table.at[layer], buffers[layer % 2], buffers[(layer + 1) % 2], rows + 2 * left, y_outs,
            top - left, height,
        )
    conv_last(last_table, buffers[(layers - 2) % 2], corrections, rows)
    copies = []
    for distance in range(1, shares):
        other = lax.rem(slab + distance, shares)
        copies.append(
            send(
                corrections.at[other], arrived.at[slab], back_send.at[distance - 1],
                back_recv.at[distance - 1], (other, coil),
            )
        )
    arrived[slab] = corrections[slab]
    finish(copies)
    for s in range(shares):
        span = slice(s * rows, (s + 1) * rows)
        for p in range(planes):
            for h in range(2):
                refined[h, p, span] = out[h, p, span] + arrived[s, 2 * p + h, :rows]


def body(sensitivity, kspace, sampling, prior_image, w_first, w_middle, w_last):
    maps, measured = sensitivity[0], kspace[0]
    planes, height, width = sampling.shape
    block = prior_image.shape[2]
    shares = lax.axis_size("slab")
    coils = lax.axis_size("coil")
    rows = block // shares
    channels = w_first.shape[0]
    layers = w_middle.shape[0] + 2
    whole = shares * planes
    y_outs = 2 if rows % 2 == 0 else 1
    cosine, sine = dft_parts(height)
    high, low = halves(np.concatenate([cosine, sine]))
    y_table = np.concatenate([high, high, low], axis=1)
    cosine, sine = dft_parts(width)
    high, low = halves(np.block([[cosine, -sine], [sine, cosine]]))
    z_table = np.concatenate([high, high, low], axis=0)
    w_first = jnp.transpose(w_first, (2, 3, 4, 1, 0))
    w_middle = jnp.transpose(w_middle, (0, 3, 4, 5, 1, 2)).reshape(layers - 2, 3, 3, 3 * channels, channels)
    w_last = jnp.transpose(w_last, (2, 3, 4, 0, 1))
    image = (2, planes, height, width)
    brick = (2, planes, block, width)
    tall = rows + -rows % 8
    deep = rows + 2 * layers
    hidden = (rows + 2 * (layers - 1), whole + 2, channels, width)
    kernel = pl.pallas_call(
        functools.partial(step_kernel, shares, coils),
        out_shape=[jax.ShapeDtypeStruct(brick, jnp.float32)] * 2,
        in_specs=[pl.BlockSpec(memory_space=pltpu.VMEM)] * 9,
        out_specs=[pl.BlockSpec(memory_space=pltpu.VMEM)] * 2,
        scratch_shapes=[
            pltpu.VMEM((2,) + image, jnp.float32),
            pltpu.VMEM((3, planes, height, width), jnp.int32),
            pltpu.VMEM((3, coils - 1, planes, block, width), jnp.int32),
            pltpu.VMEM(brick, jnp.float32),
            pltpu.VMEM(image, jnp.float32),
            pltpu.VMEM(brick, jnp.float32),
            pltpu.VMEM(image, jnp.bfloat16),
            pltpu.VMEM((2, 1, 128), jnp.float32),
            pltpu.VMEM((2, shares * coils - 1, 1, 128), jnp.float32),
            pltpu.VMEM((2, block + 2 * layers, 2 * planes, width), jnp.float32),
            pltpu.VMEM((2, deep, shares + 2, 2 * planes, width), jnp.float32),
            pltpu.VMEM((56, 128), jnp.float32),
            pltpu.VMEM((8 * channels, 256), jnp.bfloat16),
            pltpu.VMEM((layers - 2, 2 * y_outs * 3 * channels, (y_outs + 2) * 4 * channels), jnp.bfloat16),
            pltpu.VMEM((12 * tall, (rows + 2) * 4 * channels), jnp.bfloat16),
            pltpu.VMEM((deep, 80, whole // 8 * width), jnp.bfloat16),
            pltpu.VMEM(hidden, jnp.bfloat16),
            pltpu.VMEM(hidden, jnp.bfloat16),
            pltpu.VMEM((shares, 2 * planes, tall, width), jnp.float32),
            pltpu.VMEM((shares, 2 * planes, tall, width), jnp.float32),
            pltpu.SemaphoreType.DMA((4, planes, coils - 1)),
            pltpu.SemaphoreType.DMA((4, planes, coils - 1)),
            pltpu.SemaphoreType.DMA((2, shares * coils - 1)),
            pltpu.SemaphoreType.DMA((2, shares * coils - 1)),
            pltpu.SemaphoreType.DMA((2, 2)),
            pltpu.SemaphoreType.DMA((2, 2)),
            pltpu.SemaphoreType.DMA((2, shares - 1)),
            pltpu.SemaphoreType.DMA((2, shares - 1)),
            pltpu.SemaphoreType.DMA((shares - 1,)),
            pltpu.SemaphoreType.DMA((shares - 1,)),
        ],
        compiler_params=pltpu.CompilerParams(
            collective_id=0, has_side_effects=True, vmem_limit_bytes=56 * 1024 * 1024
        ),
    )
    return tuple(kernel(maps, measured, sampling, prior_image, y_table, z_table, w_first, w_middle, w_last))


def solution(mesh):
    placed = (
        P("coil", None, "slab", None, None),
        P("coil", None, "slab", None, None),
        P("slab", None, None),
        P(None, "slab", "coil", None),
        P(),
        P(),
        P(),
    )
    return jax.shard_map(
        body,
        mesh=mesh,
        in_specs=placed,
        out_specs=(P(None, "slab", "coil", None), P(None, "slab", "coil", None)),
        check_vma=False,
    )
```

```python
import functools

import jax
import jax.numpy as jnp
import numpy as np
from jax import lax
from jax.experimental import pallas as pl
from jax.experimental.pallas import tpu as pltpu
from jax.sharding import PartitionSpec as P

LAMBDA = 0.5
MESH = pl.DeviceIdType.MESH


def dft_parts(length):
    positions = np.arange(length)
    angles = 2.0 * np.pi / length * (positions[:, None] * positions[None, :] % length)
    return np.cos(angles) / np.sqrt(length), np.sin(angles) / np.sqrt(length)


def halves(table):
    table = table.astype(np.float32)
    high = table.astype(jnp.bfloat16)
    low = (table - high.astype(np.float32)).astype(jnp.bfloat16)
    return high, low


def split(values):
    high = values.astype(jnp.bfloat16)
    return high, (values - high.astype(jnp.float32)).astype(jnp.bfloat16)


def multiply(left, right):
    return jnp.dot(left, right, preferred_element_type=jnp.float32)


def transform(real, imag, y_table, z_table):
    rows, width = real.shape
    high, low = split(jnp.concatenate([real, imag], axis=1))
    field = multiply(y_table[...], jnp.concatenate([high, low, high], axis=0))
    field = jnp.concatenate(
        [field[:rows, :width] + field[rows:, width:], field[:rows, width:] - field[rows:, :width]], axis=1
    )
    high, low = split(field)
    field = multiply(jnp.concatenate([high, low, high], axis=1), z_table[...])
    return field[:, :width], field[:, width:]


def total_of(values):
    return jnp.sum(jnp.sum(values, axis=0, keepdims=True), axis=1, keepdims=True)


BIAS = 128
LOW_HALF = 65535


def pack(real, imag):
    largest = jnp.maximum(
        jnp.max(jnp.abs(real), axis=0, keepdims=True), jnp.max(jnp.abs(imag), axis=0, keepdims=True)
    )
    exponent = jnp.maximum(jnp.ceil(jnp.log2(jnp.maximum(largest, 1e-35)) - 14.98), -110.0)
    scale = jnp.exp2(-exponent)
    real = jnp.round(real * scale).astype(jnp.int32)
    imag = jnp.round(imag * scale).astype(jnp.int32)
    code = exponent.astype(jnp.int32) + BIAS
    places = lax.broadcasted_iota(jnp.int32, (8, real.shape[1]), 0)
    bits = jnp.bitwise_and(jnp.right_shift(jnp.broadcast_to(code, places.shape), places), 1)
    head = jnp.bitwise_or(jnp.bitwise_and(real[:8], -2), bits)
    real = jnp.concatenate([head, real[8:]], axis=0)
    return jnp.bitwise_or(jnp.left_shift(real, 16), jnp.bitwise_and(imag, LOW_HALF))


def unpack(words):
    real = jnp.right_shift(words, 16)
    imag = jnp.right_shift(jnp.left_shift(words, 16), 16)
    places = lax.broadcasted_iota(jnp.int32, (8, words.shape[1]), 0)
    bits = jnp.left_shift(jnp.bitwise_and(real[:8], 1), places)
    code = jnp.sum(bits, axis=0, keepdims=True)
    scale = jnp.exp2((code - BIAS).astype(jnp.float32))
    return real.astype(jnp.float32) * scale, imag.astype(jnp.float32) * scale


def spread(blocks, x_out):
    empty = jnp.zeros_like(blocks[0])
    return jnp.concatenate([empty] * x_out + blocks + [empty] * (1 - x_out), axis=1)


def first_weights(taps, base, table):
    outs = taps.shape[-1]
    for u in range(3):
        for v in range(3):
            for t in range(3):
                index = ((v * 3 + t) * 3 + u) * 2
                base[index : index + 2, :outs] = taps[u, v, t].astype(jnp.float32)
    window = (24, table.shape[0])
    row = lax.broadcasted_iota(jnp.int32, window, 0)
    place = row - 2 * (lax.broadcasted_iota(jnp.int32, window, 1) // outs) - 2
    rest = jnp.zeros((8, window[1]), jnp.float32)
    blocks = []
    for v in range(3):
        for t in range(3):
            block = jnp.zeros(window, jnp.float32)
            for k in range(6):
                index = (v * 3 + t) * 6 + k
                line = jnp.concatenate([base[index : index + 1, :outs]] * (window[1] // outs), axis=1)
                block = jnp.where(place == k, line, block)
            blocks.append(block)
        blocks.append(rest)
    blocks.append(jnp.zeros((16, window[1]), jnp.float32))
    table[...] = jnp.transpose(jnp.concatenate(blocks, axis=0)).astype(table.dtype)


def middle_weights(taps, table, y_outs):
    count, channels = taps.shape[3:]
    span = 4 * channels
    table[...] = jnp.zeros(table.shape, table.dtype)
    for layer in range(taps.shape[0]):
        for v in range(3):
            for x_out in range(2):
                block = spread([taps[layer, u, v] for u in range(3)], x_out)
                for y_out in range(y_outs):
                    base = (x_out * y_outs + y_out) * count
                    y_in = y_out + v
                    table[layer, base : base + count, y_in * span : (y_in + 1) * span] = block


def last_weights(taps, table, tall):
    channels = taps.shape[-1]
    span = 4 * channels
    row = lax.broadcasted_iota(jnp.int32, (tall, span), 0)
    for t in range(3):
        for x_out in range(2):
            lines = [spread([taps[u, v, t].astype(jnp.float32) for u in range(3)], x_out) for v in range(3)]
            for o in range(2):
                base = ((t * 2 + x_out) * 2 + o) * tall
                for y_in in range(table.shape[1] // span):
                    block = jnp.zeros((tall, span), jnp.float32)
                    for v in range(3):
                        block = jnp.where(row == y_in - v, lines[v][o : o + 1], block)
                    table[base : base + tall, y_in * span : (y_in + 1) * span] = block.astype(table.dtype)


def along_z(before, centre, after, lanes):
    width = centre.shape[1]
    before = jnp.where(lanes == 0, 0.0, pltpu.roll(before, 1, 1))
    after = jnp.where(lanes == width - 1, 0.0, pltpu.roll(after, width - 1, 1))
    return centre + before + after


def conv_first(table, taken, sink, rows, top, height):
    outs = sink.shape[2]
    width = sink.shape[3]
    depth = 3 * taken.shape[1]
    for y in range(rows):
        inside = jnp.logical_and(top + y >= 0, top + y < height)
        product = multiply(table[:, :depth], taken[y : y + 3].reshape(depth, taken.shape[2]))
        for group in range(taken.shape[2] // width):
            for q in range(table.shape[0] // outs):
                value = product[q * outs : (q + 1) * outs, group * width : (group + 1) * width]
                value = jnp.where(inside, jnp.maximum(value, 0.0), 0.0)
                sink[y, group * (table.shape[0] // outs) + q + 1] = value.astype(jnp.bfloat16)


def conv_middle(table, source, sink, rows, y_outs, top, height):
    planes, outs, width = source.shape[1] - 2, source.shape[2], source.shape[3]
    lanes = lax.broadcasted_iota(jnp.int32, (outs, width), 1)
    depth = (y_outs + 2) * 4 * outs
    group = 2 if planes % 4 == 0 else 1
    for y in range(0, rows, y_outs):
        for first in range(0, planes, 2 * group):
            taken = [
                source[y : y + y_outs + 2, first + 2 * k : first + 2 * k + 4].reshape(depth, width)
                for k in range(group)
            ]
            product = multiply(table[...], jnp.concatenate(taken, axis=1))
            for x_out in range(2):
                for y_out in range(y_outs):
                    base = (x_out * y_outs + y_out) * 3 * outs
                    inside = jnp.logical_and(top + y + y_out >= 0, top + y + y_out < height)
                    for k in range(group):
                        parts = [
                            product[base + t * outs : base + (t + 1) * outs, k * width : (k + 1) * width]
                            for t in range(3)
                        ]
                        value = along_z(*parts, lanes)
                        value = jnp.where(inside, jnp.maximum(value, 0.0), 0.0)
                        sink[y + y_out, first + 2 * k + x_out + 1] = value.astype(jnp.bfloat16)


def conv_last(table, source, sink, rows, order, ready):
    channels, width = source.shape[2], source.shape[3]
    tall = table.shape[0] // 3
    lanes = lax.broadcasted_iota(jnp.int32, (tall, width), 1)
    depth = (rows + 2) * 4 * channels
    for first in range(0, len(order), 2):
        targets = order[first : first + 2]
        taken = [source[: rows + 2, pl.ds(2 * target, 4)].reshape(depth, width) for target in targets]
        product = multiply(table[...], jnp.concatenate(taken, axis=1))
        for k, target in enumerate(targets):
            parts = [product[t * tall : (t + 1) * tall, k * width : (k + 1) * width] for t in range(3)]
            sink[target] = along_z(*parts, lanes).reshape(sink.shape[1:])
        for k, target in enumerate(targets):
            ready(first + k, target)


def step_kernel(
    shares, coils, *refs,
):
    outside, (half, correction), refs = refs[:9], refs[9:11], refs[11:]
    inside, load_sem, refs = refs[:9], refs[9], refs[10:]
    maps, measured, mask, prior, y_table, z_table, w_first, w_middle, w_last = inside
    (
        part, outbox, inbox, own_rhs, rhs, own_residual, residual, note, notes, fields, taken_fields,
        base, first_table, middle_table, last_table, shifted, even, odd, corrections, arrived,
        block_send, block_recv, note_send, note_recv, edge_send, edge_recv, field_send, field_recv, back_send, back_recv,
    ) = refs
    loads = [
        pltpu.make_async_copy(source, target, load_sem.at[index])
        for index, (source, target) in enumerate(zip(outside, inside))
    ]
    for index in (1, 2, 4, 5, 0, 6, 8, 3, 7):
        loads[index].start()
    slab = lax.axis_index("slab")
    coil = lax.axis_index("coil")
    devices = shares * coils
    me = slab * coils + coil
    planes = maps.shape[1]
    height, width = maps.shape[2:]
    block = prior.shape[2]
    rows = block // shares
    layers = w_middle.shape[0] + 2
    halo = layers
    y_outs = 2 if rows % 2 == 0 else 1
    tables = (y_table, z_table)

    def device_at(distance):
        other = lax.rem(me + distance, devices)
        return (other // coils, lax.rem(other, coils))

    barrier = pltpu.get_barrier_semaphore()
    for distance in range(1, devices):
        pl.semaphore_signal(barrier, inc=1, device_id=device_at(distance), device_id_type=MESH)

    def rows_of(index):
        return pl.ds(pl.multiple_of(index * block, block), block)

    mine = rows_of(coil)

    def send(source, target, send_sem, recv_sem, device):
        copy = pltpu.make_async_remote_copy(
            src_ref=source, dst_ref=target, send_sem=send_sem, recv_sem=recv_sem,
            device_id=device, device_id_type=MESH,
        )
        copy.start()
        return copy

    def to_coils(phase, p, source, target):
        copies = []
        for distance in range(1, coils):
            other = lax.rem(coil + distance, coils)
            copies.append(
                send(
                    source(other), target(distance), block_send.at[phase, p, distance - 1],
                    block_recv.at[phase, p, distance - 1], (slab, other),
                )
            )
        return copies

    def scatter(phase, p):
        return to_coils(
            phase, p, lambda other: outbox.at[phase, p, rows_of(other)],
            lambda distance: inbox.at[phase, distance - 1, p],
        )

    def gather_rhs(p):
        return to_coils(
            2, p, lambda other: outbox.at[2, p, pl.ds(0, block)], lambda distance: inbox.at[2, distance - 1, p]
        )

    def gather(p):
        return to_coils(
            3, p, lambda other: residual.at[:, p, mine], lambda distance: residual.at[:, p, mine]
        )

    def tell(phase):
        for distance in range(1, devices):
            send(
                note.at[phase], notes.at[phase, distance - 1], note_send.at[phase], note_recv.at[phase],
                device_at(distance),
            )
        return pltpu.make_async_remote_copy(
            src_ref=notes.at[phase], dst_ref=notes.at[phase], send_sem=note_send.at[phase],
            recv_sem=note_recv.at[phase], device_id=device_at(1), device_id_type=MESH,
        )

    def send_edges(which):
        above = lax.rem(coil + coils - 1, coils)
        below = lax.rem(coil + 1, coils)
        ends = ((block, 0, below), (halo, halo + block, above))
        return [
            send(
                fields.at[which, pl.ds(source, halo)], fields.at[which, pl.ds(target, halo)],
                edge_send.at[which, side], edge_recv.at[which, side], (slab, other),
            )
            for side, (source, target, other) in enumerate(ends)
        ]

    deep = rows + 2 * halo

    def send_fields(which, copies):
        finish(copies)
        top_edge = fields[which, :halo]
        fields[which, :halo] = jnp.where(coil > 0, top_edge, 0.0)
        low_edge = fields[which, halo + block :]
        fields[which, halo + block :] = jnp.where(coil < coils - 1, low_edge, 0.0)
        copies = []
        for distance in range(1, shares):
            other = lax.rem(slab + distance, shares)
            copies.append(
                send(
                    fields.at[which, pl.ds(other * rows, deep)], taken_fields.at[which, :, slab + 1],
                    field_send.at[which, distance - 1], field_recv.at[which, distance - 1], (other, coil),
                )
            )
        taken_fields[which, :, slab + 1] = fields[which, pl.ds(slab * rows, deep)]
        return copies

    sent = []

    def finish(copies):
        for copy in copies:
            copy.wait_recv()
        sent.extend(copies)

    lanes = lax.broadcasted_iota(jnp.int32, (1, note.shape[2]), 1)

    def write_note(phase, values):
        line = jnp.zeros(lanes.shape, jnp.float32)
        for index, value in enumerate(values):
            line = jnp.where(lanes == index, value, line)
        note[phase] = line

    def read_notes(phase, count):
        line = note[phase]
        for distance in range(1, devices):
            line = line + notes[phase, distance - 1]
        return [jnp.sum(jnp.where(lanes == index, line, 0.0), axis=1, keepdims=True) for index in range(count)]

    def backward_part(real, imag, phase, p):
        imag, real = transform(imag, real, *tables)
        part_re = maps[0, p] * real + maps[1, p] * imag
        part_im = maps[0, p] * imag - maps[1, p] * real
        part[phase, 0, p] = part_re
        part[phase, 1, p] = part_im
        for index in range(coils):
            span = slice(index * block, (index + 1) * block)
            outbox[phase, p, span] = pack(part_re[span], part_im[span])

    def forward(image_re, image_im, p):
        real = maps[0, p] * image_re - maps[1, p] * image_im
        imag = maps[0, p] * image_im + maps[1, p] * image_re
        real, imag = transform(real, imag, *tables)
        sampled = mask[p].astype(jnp.float32)
        return real * sampled, imag * sampled

    def reduced(phase, p):
        real = part[phase, 0, p, mine]
        imag = part[phase, 1, p, mine]
        for distance in range(1, coils):
            more = unpack(inbox[phase, distance - 1, p])
            real = real + more[0]
            imag = imag + more[1]
        return real, imag

    pending = []
    for index in (1, 2, 4, 5, 0):
        loads[index].wait()
    for p in range(planes):
        sampled = mask[p].astype(jnp.float32)
        backward_part(measured[0, p] * sampled, measured[1, p] * sampled, 0, p)
        if p == 0:
            pl.semaphore_wait(barrier, devices - 1)
        pending.append(scatter(0, p))
    for index in (6, 8, 3, 7):
        loads[index].wait()
    first_weights(w_first, base, first_table)
    last_weights(w_last, last_table, last_table.shape[0] // 12)
    total = taken_fields.shape[2]
    for which in range(2):
        for outer in (0, total - 1):
            taken_fields[which, :, outer] = jnp.zeros((deep,) + taken_fields.shape[3:], jnp.float32)
    shifted[...] = jnp.zeros(shifted.shape, shifted.dtype)
    for buffer in (even, odd):
        for outer in (0, buffer.shape[1] - 1):
            buffer[:, outer] = jnp.zeros((buffer.shape[0],) + buffer.shape[2:], buffer.dtype)
    gathers = []
    norm = jnp.zeros((1, 1), jnp.float32)
    for p in range(planes):
        finish(pending[p])
        real, imag = reduced(0, p)
        real = real + LAMBDA * prior[0, p]
        imag = imag + LAMBDA * prior[1, p]
        outbox[2, p, :block] = pack(real, imag)
        gathers.append(gather_rhs(p))
        for h, value in enumerate((real, imag)):
            own_rhs[h, p] = value
            rhs[h, p, mine] = value
            fields[0, halo : halo + block, 2 * p + h] = value
            norm = norm + total_of(value * value)
    edge_copies = send_edges(0)
    middle_weights(w_middle, middle_table, y_outs)
    energy = LAMBDA * norm
    pending = []
    for p in range(planes):
        finish(gathers[p])
        for distance in range(1, coils):
            source = rows_of(lax.rem(coil + coils - distance, coils))
            real, imag = unpack(inbox[2, distance - 1, p])
            rhs[0, p, source] = real
            rhs[1, p, source] = imag
        real, imag = forward(rhs[0, p], rhs[1, p], p)
        energy = energy + total_of(real * real) + total_of(imag * imag)
        if p == planes - 1:
            write_note(0, [norm, energy])
            first_notes = tell(0)
        backward_part(real, imag, 1, p)
        pending.append(scatter(1, p))
    field_copies = send_fields(0, edge_copies)
    first_notes.wait_recv()
    norm, curvature = read_notes(0, 2)
    step = norm / curvature
    gathers = []
    norm_next = jnp.zeros((1, 1), jnp.float32)
    cross = jnp.zeros((1, 1), jnp.float32)
    for p in range(planes):
        finish(pending[p])
        images = reduced(1, p)
        for h in range(2):
            direction = own_rhs[h, p]
            image = images[h] + LAMBDA * direction
            value = direction - step * image
            own_residual[h, p] = value
            residual[h, p, mine] = value.astype(jnp.bfloat16)
            fields[1, halo : halo + block, 2 * p + h] = value
        gathers.append(gather(p))
        for h in range(2):
            value = own_residual[h, p]
            image = images[h] + LAMBDA * own_rhs[h, p]
            norm_next = norm_next + total_of(value * value)
            cross = cross + total_of(value * image)
    edge_copies = send_edges(1)
    energy = LAMBDA * norm_next
    for p in range(planes):
        finish(gathers[p])
        if p == planes - 1:
            field_copies = field_copies + send_fields(1, edge_copies)
        real, imag = forward(residual[0, p].astype(jnp.float32), residual[1, p].astype(jnp.float32), p)
        energy = energy + total_of(real * real) + total_of(imag * imag)
    write_note(1, [norm_next, energy, cross])
    last_notes = tell(1)
    finish(field_copies)
    last_notes.wait_recv()
    norm_next, energy, cross = read_notes(1, 3)
    ratio = norm_next / norm
    curvature = energy + 2.0 * ratio * cross + ratio * ratio * curvature
    step_next = norm_next / curvature
    share = step + step_next * ratio
    across = lax.broadcasted_iota(jnp.int32, (4 * total, width), 1)
    for y in range(deep):
        line = share * taken_fields[0, y].reshape(4 * total, width)
        line = line + step_next * taken_fields[1, y].reshape(4 * total, width)
        line = line.astype(jnp.bfloat16).astype(jnp.float32)
        before = jnp.where(across == 0, 0.0, pltpu.roll(line, 1, 1))
        after = jnp.where(across == width - 1, 0.0, pltpu.roll(line, width - 1, 1))
        for group in range(shifted.shape[2] // width):
            span = slice(16 * group, 16 * group + 24)
            piece = jnp.concatenate([before[span], line[span], after[span], jnp.zeros((8, width), jnp.float32)], axis=0)
            shifted[y, :, group * width : (group + 1) * width] = piece.astype(jnp.bfloat16)
    for h in range(2):
        for p in range(planes):
            half[h, p] = 0.5 * (share * own_rhs[h, p] + step_next * own_residual[h, p])
    top = coil * block + slab * rows
    left = layers - 1
    conv_first(first_table, shifted, even, rows + 2 * left, top - left, height)
    buffers = (even, odd)
    for layer in range(layers - 2):
        left = left - 1
        conv_middle(
            middle_table.at[layer], buffers[layer % 2], buffers[(layer + 1) % 2], rows + 2 * left, y_outs,
            top - left, height,
        )
    copies = []

    def give(index, other):
        if index < shares - 1:
            copies.append(
                send(
                    corrections.at[other], arrived.at[slab], back_send.at[index], back_recv.at[index], (other, coil)
                )
            )

    order = [lax.rem(slab + shares - 1 - index, shares) for index in range(shares)]
    conv_last(last_table, buffers[(layers - 2) % 2], corrections, rows, order, give)
    arrived[slab] = corrections[slab]
    for copy in sent:
        copy.wait_send()
    first_notes.wait_send()
    last_notes.wait_send()
    sent.clear()
    finish(copies)
    for copy in copies:
        copy.wait_send()
    for s in range(shares):
        span = slice(s * rows, (s + 1) * rows)
        for p in range(planes):
            for h in range(2):
                correction[h, p, span] = arrived[s, 2 * p + h, :rows]


def body(sensitivity, kspace, sampling, prior_image, w_first, w_middle, w_last):
    maps, measured = sensitivity[0], kspace[0]
    planes, height, width = sampling.shape
    block = prior_image.shape[2]
    shares = lax.axis_size("slab")
    coils = lax.axis_size("coil")
    rows = block // shares
    channels = w_first.shape[0]
    layers = w_middle.shape[0] + 2
    whole = shares * planes
    y_outs = 2 if rows % 2 == 0 else 1
    cosine, sine = dft_parts(height)
    high, low = halves(np.concatenate([cosine, sine]))
    y_table = np.concatenate([high, high, low], axis=1)
    cosine, sine = dft_parts(width)
    high, low = halves(np.block([[cosine, -sine], [sine, cosine]]))
    z_table = np.concatenate([high, high, low], axis=0)
    w_first = jnp.transpose(w_first, (2, 3, 4, 1, 0))
    w_middle = jnp.transpose(w_middle, (0, 3, 4, 5, 1, 2)).reshape(layers - 2, 3, 3, 3 * channels, channels)
    w_last = jnp.transpose(w_last, (2, 3, 4, 0, 1))
    image = (2, planes, height, width)
    brick = (2, planes, block, width)
    tall = rows + -rows % 8
    deep = rows + 2 * layers
    hidden = (rows + 2 * (layers - 1), whole + 2, channels, width)
    operands = (maps, measured, sampling, prior_image, y_table, z_table, w_first, w_middle, w_last)
    kernel = pl.pallas_call(
        functools.partial(step_kernel, shares, coils),
        out_shape=[pltpu.VMEM(brick, jnp.float32)] * 2,
        in_specs=[pl.BlockSpec(memory_space=pl.ANY)] * 9,
        out_specs=[pl.BlockSpec(memory_space=pltpu.VMEM)] * 2,
        scratch_shapes=[pltpu.VMEM(operand.shape, operand.dtype) for operand in operands]
        + [
            pltpu.SemaphoreType.DMA((len(operands),)),
            pltpu.VMEM((2,) + image, jnp.float32),
            pltpu.VMEM((3, planes, height, width), jnp.int32),
            pltpu.VMEM((3, coils - 1, planes, block, width), jnp.int32),
            pltpu.VMEM(brick, jnp.float32),
            pltpu.VMEM(image, jnp.float32),
            pltpu.VMEM(brick, jnp.float32),
            pltpu.VMEM(image, jnp.bfloat16),
            pltpu.VMEM((2, 1, 128), jnp.float32),
            pltpu.VMEM((2, shares * coils - 1, 1, 128), jnp.float32),
            pltpu.VMEM((2, block + 2 * layers, 2 * planes, width), jnp.float32),
            pltpu.VMEM((2, deep, shares + 2, 2 * planes, width), jnp.float32),
            pltpu.VMEM((56, 128), jnp.float32),
            pltpu.VMEM((8 * channels, 256), jnp.bfloat16),
            pltpu.VMEM((layers - 2, 2 * y_outs * 3 * channels, (y_outs + 2) * 4 * channels), jnp.bfloat16),
            pltpu.VMEM((12 * tall, (rows + 2) * 4 * channels), jnp.bfloat16),
            pltpu.VMEM((deep, 80, whole // 8 * width), jnp.bfloat16),
            pltpu.VMEM(hidden, jnp.bfloat16),
            pltpu.VMEM(hidden, jnp.bfloat16),
            pltpu.VMEM((shares, 2 * planes, tall, width), jnp.float32),
            pltpu.VMEM((shares, 2 * planes, tall, width), jnp.float32),
            pltpu.SemaphoreType.DMA((4, planes, coils - 1)),
            pltpu.SemaphoreType.DMA((4, planes, coils - 1)),
            pltpu.SemaphoreType.DMA((2,)),
            pltpu.SemaphoreType.DMA((2,)),
            pltpu.SemaphoreType.DMA((2, 2)),
            pltpu.SemaphoreType.DMA((2, 2)),
            pltpu.SemaphoreType.DMA((2, shares - 1)),
            pltpu.SemaphoreType.DMA((2, shares - 1)),
            pltpu.SemaphoreType.DMA((shares - 1,)),
            pltpu.SemaphoreType.DMA((shares - 1,)),
        ],
        compiler_params=pltpu.CompilerParams(
            collective_id=0, has_side_effects=True, vmem_limit_bytes=56 * 1024 * 1024
        ),
    )
    half, correction = kernel(*operands)
    image = half + half
    return image, image + correction


def solution(mesh):
    placed = (
        P("coil", None, "slab", None, None),
        P("coil", None, "slab", None, None),
        P("slab", None, None),
        P(None, "slab", "coil", None),
        P(),
        P(),
        P(),
    )
    return jax.shard_map(
        body,
        mesh=mesh,
        in_specs=placed,
        out_specs=(P(None, "slab", "coil", None), P(None, "slab", "coil", None)),
        check_vma=False,
    )
```

```python
import functools

import jax
import jax.numpy as jnp
import numpy as np
from jax import lax
from jax.experimental import pallas as pl
from jax.experimental.pallas import tpu as pltpu
from jax.sharding import PartitionSpec as P

LAMBDA = 0.5
MESH = pl.DeviceIdType.MESH


def dft_parts(length):
    positions = np.arange(length)
    angles = 2.0 * np.pi / length * (positions[:, None] * positions[None, :] % length)
    return np.cos(angles) / np.sqrt(length), np.sin(angles) / np.sqrt(length)


def halves(table):
    table = table.astype(np.float32)
    high = table.astype(jnp.bfloat16)
    low = (table - high.astype(np.float32)).astype(jnp.bfloat16)
    return high, low


def split(values):
    high = values.astype(jnp.bfloat16)
    return high, (values - high.astype(jnp.float32)).astype(jnp.bfloat16)


def multiply(left, right):
    return jnp.dot(left, right, preferred_element_type=jnp.float32)


def transform(real, imag, y_table, z_table):
    rows, width = real.shape
    high, low = split(jnp.concatenate([real, imag], axis=1))
    y_high, y_low = y_table[:, :rows], y_table[:, rows:]
    z_high, z_low = z_table[: 2 * width], z_table[2 * width :]
    field = multiply(
        jnp.concatenate([y_high, y_high, y_low], axis=1), jnp.concatenate([high, low, high], axis=0)
    )
    field = jnp.concatenate(
        [field[:rows, :width] + field[rows:, width:], field[:rows, width:] - field[rows:, :width]], axis=1
    )
    high, low = split(field)
    field = multiply(
        jnp.concatenate([high, low, high], axis=1), jnp.concatenate([z_high, z_high, z_low], axis=0)
    )
    return field[:, :width], field[:, width:]


def fold(values):
    return jnp.sum(values.reshape(values.shape[0] // 8, 8, values.shape[1]), axis=0)


def total_of(values):
    return jnp.sum(jnp.sum(values, axis=0, keepdims=True), axis=1, keepdims=True)


BIAS = 128
LOW_HALF = 65535


def pack(real, imag):
    largest = jnp.maximum(
        jnp.max(jnp.abs(real), axis=0, keepdims=True), jnp.max(jnp.abs(imag), axis=0, keepdims=True)
    )
    exponent = jnp.maximum(jnp.ceil(jnp.log2(jnp.maximum(largest, 1e-35)) - 14.98), -110.0)
    scale = jnp.exp2(-exponent)
    real = jnp.round(real * scale).astype(jnp.int32)
    imag = jnp.round(imag * scale).astype(jnp.int32)
    code = exponent.astype(jnp.int32) + BIAS
    places = lax.broadcasted_iota(jnp.int32, (8, real.shape[1]), 0)
    bits = jnp.bitwise_and(jnp.right_shift(jnp.broadcast_to(code, places.shape), places), 1)
    head = jnp.bitwise_or(jnp.bitwise_and(real[:8], -2), bits)
    real = jnp.concatenate([head, real[8:]], axis=0)
    return jnp.bitwise_or(jnp.left_shift(real, 16), jnp.bitwise_and(imag, LOW_HALF))


def unpack(words):
    real = jnp.right_shift(words, 16)
    imag = jnp.right_shift(jnp.left_shift(words, 16), 16)
    places = lax.broadcasted_iota(jnp.int32, (8, words.shape[1]), 0)
    bits = jnp.left_shift(jnp.bitwise_and(real[:8], 1), places)
    code = jnp.sum(bits, axis=0, keepdims=True)
    scale = jnp.exp2((code - BIAS).astype(jnp.float32))
    return real.astype(jnp.float32) * scale, imag.astype(jnp.float32) * scale


def spread(blocks, x_out):
    empty = jnp.zeros_like(blocks[0])
    return jnp.concatenate([empty] * x_out + blocks + [empty] * (1 - x_out), axis=1)


def first_weights(taps, base, table):
    outs = taps.shape[-1]
    for u in range(3):
        for v in range(3):
            for t in range(3):
                index = ((v * 3 + t) * 3 + u) * 2
                base[index : index + 2, :outs] = taps[u, v, t].astype(jnp.float32)
    window = (24, table.shape[0])
    row = lax.broadcasted_iota(jnp.int32, window, 0)
    place = row - 2 * (lax.broadcasted_iota(jnp.int32, window, 1) // outs) - 2
    rest = jnp.zeros((8, window[1]), jnp.float32)
    blocks = []
    for v in range(3):
        for t in range(3):
            block = jnp.zeros(window, jnp.float32)
            for k in range(6):
                index = (v * 3 + t) * 6 + k
                line = jnp.concatenate([base[index : index + 1, :outs]] * (window[1] // outs), axis=1)
                block = jnp.where(place == k, line, block)
            blocks.append(block)
        blocks.append(rest)
    blocks.append(jnp.zeros((16, window[1]), jnp.float32))
    table[...] = jnp.transpose(jnp.concatenate(blocks, axis=0)).astype(table.dtype)


def middle_weights(taps, table, y_outs):
    count, channels = taps.shape[3:]
    span = 4 * channels
    table[...] = jnp.zeros(table.shape, table.dtype)
    for layer in range(taps.shape[0]):
        for v in range(3):
            for x_out in range(2):
                block = spread([taps[layer, u, v] for u in range(3)], x_out)
                for y_out in range(y_outs):
                    base = (x_out * y_outs + y_out) * count
                    y_in = y_out + v
                    table[layer, base : base + count, y_in * span : (y_in + 1) * span] = block


def last_weights(taps, table, tall):
    channels = taps.shape[-1]
    span = 4 * channels
    row = lax.broadcasted_iota(jnp.int32, (tall, span), 0)
    for t in range(3):
        for x_out in range(2):
            lines = [spread([taps[u, v, t].astype(jnp.float32) for u in range(3)], x_out) for v in range(3)]
            for o in range(2):
                base = ((t * 2 + x_out) * 2 + o) * tall
                for y_in in range(table.shape[1] // span):
                    block = jnp.zeros((tall, span), jnp.float32)
                    for v in range(3):
                        block = jnp.where(row == y_in - v, lines[v][o : o + 1], block)
                    table[base : base + tall, y_in * span : (y_in + 1) * span] = block.astype(table.dtype)


def along_z(before, centre, after, lanes):
    width = centre.shape[1]
    before = jnp.where(lanes == 0, 0.0, pltpu.roll(before, 1, 1))
    after = jnp.where(lanes == width - 1, 0.0, pltpu.roll(after, width - 1, 1))
    return centre + before + after


def conv_first(table, taken, sink, rows, top, height):
    outs = sink.shape[2]
    width = sink.shape[3]
    depth = 3 * taken.shape[1]
    for y in range(rows):
        inside = jnp.logical_and(top + y >= 0, top + y < height)
        product = multiply(table[:, :depth], taken[y : y + 3].reshape(depth, taken.shape[2]))
        for group in range(taken.shape[2] // width):
            for q in range(table.shape[0] // outs):
                value = product[q * outs : (q + 1) * outs, group * width : (group + 1) * width]
                value = jnp.where(inside, jnp.maximum(value, 0.0), 0.0)
                sink[y, group * (table.shape[0] // outs) + q + 1] = value.astype(jnp.bfloat16)


def conv_middle(table, source, sink, rows, y_outs, top, height):
    planes, outs, width = source.shape[1] - 2, source.shape[2], source.shape[3]
    lanes = lax.broadcasted_iota(jnp.int32, (outs, width), 1)
    depth = (y_outs + 2) * 4 * outs
    group = 2 if planes % 4 == 0 else 1
    for y in range(0, rows, y_outs):
        for first in range(0, planes, 2 * group):
            taken = [
                source[y : y + y_outs + 2, first + 2 * k : first + 2 * k + 4].reshape(depth, width)
                for k in range(group)
            ]
            product = multiply(table[...], jnp.concatenate(taken, axis=1))
            for x_out in range(2):
                for y_out in range(y_outs):
                    base = (x_out * y_outs + y_out) * 3 * outs
                    inside = jnp.logical_and(top + y + y_out >= 0, top + y + y_out < height)
                    for k in range(group):
                        parts = [
                            product[base + t * outs : base + (t + 1) * outs, k * width : (k + 1) * width]
                            for t in range(3)
                        ]
                        value = along_z(*parts, lanes)
                        value = jnp.where(inside, jnp.maximum(value, 0.0), 0.0)
                        sink[y + y_out, first + 2 * k + x_out + 1] = value.astype(jnp.bfloat16)


def conv_last(table, source, sink, rows, order, ready):
    channels, width = source.shape[2], source.shape[3]
    tall = table.shape[0] // 3
    lanes = lax.broadcasted_iota(jnp.int32, (tall, width), 1)
    depth = (rows + 2) * 4 * channels
    for first in range(0, len(order), 2):
        targets = order[first : first + 2]
        taken = [source[: rows + 2, pl.ds(2 * target, 4)].reshape(depth, width) for target in targets]
        product = multiply(table[...], jnp.concatenate(taken, axis=1))
        for k, target in enumerate(targets):
            parts = [product[t * tall : (t + 1) * tall, k * width : (k + 1) * width] for t in range(3)]
            sink[target] = along_z(*parts, lanes).reshape(sink.shape[1:])
        for k, target in enumerate(targets):
            ready(first + k, target)


def step_kernel(
    shares, coils, *refs,
):
    outside, (half, correction), refs = refs[:9], refs[9:11], refs[11:]
    inside, load_sem, refs = refs[:9], refs[9], refs[10:]
    maps, measured, mask, prior, y_table, z_table, w_first, w_middle, w_last = inside
    (
        part, outbox, inbox, own_rhs, rhs, own_image, residual, note, notes, fields, taken_fields,
        base, first_table, middle_table, last_table, shifted, even, odd, corrections, arrived,
        block_send, block_recv, note_send, note_recv, edge_send, edge_recv, field_send, field_recv, back_send, back_recv,
    ) = refs
    loads = [
        pltpu.make_async_copy(source, target, load_sem.at[index])
        for index, (source, target) in enumerate(zip(outside, inside))
    ]
    for index in (1, 2, 4, 5, 0, 6, 8, 3, 7):
        loads[index].start()
    slab = lax.axis_index("slab")
    coil = lax.axis_index("coil")
    devices = shares * coils
    planes = maps.shape[1]
    height, width = maps.shape[2:]
    block = prior.shape[2]
    rows = block // shares
    layers = w_middle.shape[0] + 2
    halo = layers
    y_outs = 2 if rows % 2 == 0 else 1
    tables = (y_table, z_table)

    offsets = [(s, c) for s in range(shares) for c in range(coils) if s or c]
    offsets.sort(key=lambda offset: -min(offset[1], coils - offset[1]) - bin(offset[0] // 2).count("1"))

    def device_at(distance):
        far_slab, far_coil = offsets[distance - 1]
        return (lax.rem(slab + far_slab, shares), lax.rem(coil + far_coil, coils))

    barrier = pltpu.get_barrier_semaphore()
    for distance in range(1, devices):
        pl.semaphore_signal(barrier, inc=1, device_id=device_at(distance), device_id_type=MESH)

    def rows_of(index):
        return pl.ds(pl.multiple_of(index * block, block), block)

    mine = rows_of(coil)

    def send(source, target, send_sem, recv_sem, device):
        copy = pltpu.make_async_remote_copy(
            src_ref=source, dst_ref=target, send_sem=send_sem, recv_sem=recv_sem,
            device_id=device, device_id_type=MESH,
        )
        copy.start()
        return copy

    def to_coils(phase, p, source, target):
        copies = []
        for distance in range(1, coils):
            other = lax.rem(coil + distance, coils)
            copies.append(
                send(
                    source(other), target(distance), block_send.at[phase, p, distance - 1],
                    block_recv.at[phase, p, distance - 1], (slab, other),
                )
            )
        return copies

    def scatter(phase, p):
        return to_coils(
            phase, p, lambda other: outbox.at[phase, p, rows_of(other)],
            lambda distance: inbox.at[phase, distance - 1, p],
        )

    def gather(phase, p):
        return to_coils(
            phase, p, lambda other: outbox.at[phase, p, pl.ds(0, block)],
            lambda distance: inbox.at[phase, distance - 1, p],
        )

    def tell(phase):
        for distance in range(1, devices):
            send(
                note.at[phase], notes.at[phase, distance - 1], note_send.at[phase], note_recv.at[phase],
                device_at(distance),
            )
        return pltpu.make_async_remote_copy(
            src_ref=notes.at[phase], dst_ref=notes.at[phase], send_sem=note_send.at[phase],
            recv_sem=note_recv.at[phase], device_id=device_at(1), device_id_type=MESH,
        )

    def send_edges(which):
        above = lax.rem(coil + coils - 1, coils)
        below = lax.rem(coil + 1, coils)
        ends = ((block, 0, below), (halo, halo + block, above))
        return [
            send(
                fields.at[which, pl.ds(source, halo)], fields.at[which, pl.ds(target, halo)],
                edge_send.at[which, side], edge_recv.at[which, side], (slab, other),
            )
            for side, (source, target, other) in enumerate(ends)
        ]

    deep = rows + 2 * halo

    def send_fields(which, copies):
        finish(copies)
        top_edge = fields[which, :halo]
        fields[which, :halo] = jnp.where(coil > 0, top_edge, 0.0)
        low_edge = fields[which, halo + block :]
        fields[which, halo + block :] = jnp.where(coil < coils - 1, low_edge, 0.0)
        copies = []
        for distance in range(1, shares):
            other = lax.rem(slab + distance, shares)
            copies.append(
                send(
                    fields.at[which, pl.ds(other * rows, deep)], taken_fields.at[which, :, slab + 1],
                    field_send.at[which, distance - 1], field_recv.at[which, distance - 1], (other, coil),
                )
            )
        taken_fields[which, :, slab + 1] = fields[which, pl.ds(slab * rows, deep)]
        return copies

    sent = []

    def finish(copies):
        for copy in copies:
            copy.wait_recv()
        sent.extend(copies)

    lanes = lax.broadcasted_iota(jnp.int32, (1, note.shape[2]), 1)

    def write_note(phase, values):
        line = jnp.zeros(lanes.shape, jnp.float32)
        for index, value in enumerate(values):
            line = jnp.where(lanes == index, value, line)
        note[phase] = line

    def read_notes(phase, count):
        line = note[phase]
        for distance in range(1, devices):
            line = line + notes[phase, distance - 1]
        return [jnp.sum(jnp.where(lanes == index, line, 0.0), axis=1, keepdims=True) for index in range(count)]

    def backward_part(real, imag, phase, p):
        imag, real = transform(imag, real, *tables)
        part_re = maps[0, p] * real + maps[1, p] * imag
        part_im = maps[0, p] * imag - maps[1, p] * real
        part[phase, 0, p] = part_re
        part[phase, 1, p] = part_im
        for index in range(coils):
            span = slice(index * block, (index + 1) * block)
            outbox[phase, p, span] = pack(part_re[span], part_im[span])

    def forward(image_re, image_im, p):
        real = maps[0, p] * image_re - maps[1, p] * image_im
        imag = maps[0, p] * image_im + maps[1, p] * image_re
        real, imag = transform(real, imag, *tables)
        sampled = mask[p].astype(jnp.float32)
        return real * sampled, imag * sampled

    def reduced(phase, p):
        real = part[phase, 0, p, mine]
        imag = part[phase, 1, p, mine]
        for distance in range(1, coils):
            more = unpack(inbox[phase, distance - 1, p])
            real = real + more[0]
            imag = imag + more[1]
        return real, imag

    pending = []
    for index in (1, 2, 4, 5, 0):
        loads[index].wait()
    for p in range(planes):
        sampled = mask[p].astype(jnp.float32)
        backward_part(measured[0, p] * sampled, measured[1, p] * sampled, 0, p)
        if p == 0:
            pl.semaphore_wait(barrier, devices - 1)
        pending.append(scatter(0, p))
    for index in (6, 8, 3, 7):
        loads[index].wait()
    first_weights(w_first, base, first_table)
    last_weights(w_last, last_table, last_table.shape[0] // 12)
    total = taken_fields.shape[2]
    for which in range(2):
        for outer in (0, total - 1):
            taken_fields[which, :, outer] = jnp.zeros((deep,) + taken_fields.shape[3:], jnp.float32)
    shifted[...] = jnp.zeros(shifted.shape, shifted.dtype)
    for buffer in (even, odd):
        for outer in (0, buffer.shape[1] - 1):
            buffer[:, outer] = jnp.zeros((buffer.shape[0],) + buffer.shape[2:], buffer.dtype)
    gathers = []
    norm = jnp.zeros((8, width), jnp.float32)
    for p in range(planes):
        finish(pending[p])
        real, imag = reduced(0, p)
        real = real + LAMBDA * prior[0, p]
        imag = imag + LAMBDA * prior[1, p]
        outbox[2, p, :block] = pack(real, imag)
        gathers.append(gather(2, p))
        for h, value in enumerate((real, imag)):
            own_rhs[h, p] = value
            rhs[h, p, mine] = value
            fields[0, halo : halo + block, 2 * p + h] = value
            norm = norm + fold(value * value)
    edge_copies = send_edges(0)
    middle_weights(w_middle, middle_table, y_outs)
    energy = LAMBDA * norm
    pending = []
    for p in range(planes):
        finish(gathers[p])
        for distance in range(1, coils):
            source = rows_of(lax.rem(coil + coils - distance, coils))
            real, imag = unpack(inbox[2, distance - 1, p])
            rhs[0, p, source] = real
            rhs[1, p, source] = imag
        real, imag = forward(rhs[0, p], rhs[1, p], p)
        energy = energy + fold(real * real + imag * imag)
        backward_part(real, imag, 1, p)
        pending.append(scatter(1, p))
    write_note(0, [total_of(norm), total_of(energy)])
    first_notes = tell(0)
    field_copies = send_fields(0, edge_copies)
    gathers = []
    for p in range(planes):
        finish(pending[p])
        images = reduced(1, p)
        images = [images[h] + LAMBDA * own_rhs[h, p] for h in range(2)]
        outbox[3, p, :block] = pack(*images)
        if p < planes - 1:
            gathers.append(gather(3, p))
        for h in range(2):
            own_image[h, p] = images[h]
            fields[1, halo : halo + block, 2 * p + h] = images[h]
    edge_copies = send_edges(1)
    gathers.append(gather(3, planes - 1))
    first_notes.wait_recv()
    norm, curvature = read_notes(0, 2)
    step = norm / curvature
    norm_next = jnp.zeros((8, width), jnp.float32)
    cross = jnp.zeros((8, width), jnp.float32)
    for p in range(planes):
        for h in range(2):
            image = own_image[h, p]
            value = own_rhs[h, p] - step * image
            norm_next = norm_next + fold(value * value)
            cross = cross + fold(value * image)
    energy = LAMBDA * norm_next
    norm_next, cross = total_of(norm_next), total_of(cross)
    for p in range(planes):
        finish(gathers[p])
        if p == 0:
            field_copies = field_copies + send_fields(1, edge_copies)
        for h in range(2):
            residual[h, mine] = own_rhs[h, p] - step * own_image[h, p]
        for distance in range(1, coils):
            source = rows_of(lax.rem(coil + coils - distance, coils))
            for h, value in enumerate(unpack(inbox[3, distance - 1, p])):
                residual[h, source] = rhs[h, p, source] - step * value
        real, imag = forward(residual[0], residual[1], p)
        energy = energy + fold(real * real + imag * imag)
    write_note(1, [norm_next, total_of(energy), cross])
    last_notes = tell(1)
    finish(field_copies)
    last_notes.wait_recv()
    norm_next, energy, cross = read_notes(1, 3)
    ratio = norm_next / norm
    curvature = energy + 2.0 * ratio * cross + ratio * ratio * curvature
    step_next = norm_next / curvature
    share = step + step_next * (1.0 + ratio)
    share_image = -step_next * step
    across = lax.broadcasted_iota(jnp.int32, (4 * total, width), 1)
    for y in range(deep):
        line = share * taken_fields[0, y].reshape(4 * total, width)
        line = line + share_image * taken_fields[1, y].reshape(4 * total, width)
        line = line.astype(jnp.bfloat16).astype(jnp.float32)
        before = jnp.where(across == 0, 0.0, pltpu.roll(line, 1, 1))
        after = jnp.where(across == width - 1, 0.0, pltpu.roll(line, width - 1, 1))
        for group in range(shifted.shape[2] // width):
            span = slice(16 * group, 16 * group + 24)
            piece = jnp.concatenate([before[span], line[span], after[span], jnp.zeros((8, width), jnp.float32)], axis=0)
            shifted[y, :, group * width : (group + 1) * width] = piece.astype(jnp.bfloat16)
    for h in range(2):
        for p in range(planes):
            half[h, p] = 0.5 * (share * own_rhs[h, p] + share_image * own_image[h, p])
    top = coil * block + slab * rows
    left = layers - 1
    conv_first(first_table, shifted, even, rows + 2 * left, top - left, height)
    buffers = (even, odd)
    for layer in range(layers - 2):
        left = left - 1
        conv_middle(
            middle_table.at[layer], buffers[layer % 2], buffers[(layer + 1) % 2], rows + 2 * left, y_outs,
            top - left, height,
        )
    copies = []

    def give(index, other):
        if index < shares - 1:
            copies.append(
                send(
                    corrections.at[other], arrived.at[slab], back_send.at[index], back_recv.at[index], (other, coil)
                )
            )

    order = [lax.rem(slab + shares - 1 - index, shares) for index in range(shares)]
    conv_last(last_table, buffers[(layers - 2) % 2], corrections, rows, order, give)
    arrived[slab] = corrections[slab]
    for copy in sent:
        copy.wait_send()
    first_notes.wait_send()
    last_notes.wait_send()
    sent.clear()
    finish(copies)
    for copy in copies:
        copy.wait_send()
    for s in range(shares):
        span = slice(s * rows, (s + 1) * rows)
        for p in range(planes):
            for h in range(2):
                correction[h, p, span] = arrived[s, 2 * p + h, :rows]


def body(sensitivity, kspace, sampling, prior_image, w_first, w_middle, w_last):
    maps, measured = sensitivity[0], kspace[0]
    planes, height, width = sampling.shape
    block = prior_image.shape[2]
    shares = lax.axis_size("slab")
    coils = lax.axis_size("coil")
    rows = block // shares
    channels = w_first.shape[0]
    layers = w_middle.shape[0] + 2
    whole = shares * planes
    y_outs = 2 if rows % 2 == 0 else 1
    cosine, sine = dft_parts(height)
    high, low = halves(np.concatenate([cosine, sine]))
    y_table = np.concatenate([high, low], axis=1)
    cosine, sine = dft_parts(width)
    high, low = halves(np.block([[cosine, -sine], [sine, cosine]]))
    z_table = np.concatenate([high, low], axis=0)
    w_first = jnp.transpose(w_first, (2, 3, 4, 1, 0))
    w_middle = jnp.transpose(w_middle, (0, 3, 4, 5, 1, 2)).reshape(layers - 2, 3, 3, 3 * channels, channels)
    w_last = jnp.transpose(w_last, (2, 3, 4, 0, 1))
    image = (2, planes, height, width)
    brick = (2, planes, block, width)
    tall = rows + -rows % 8
    deep = rows + 2 * layers
    hidden = (rows + 2 * (layers - 1), whole + 2, channels, width)
    operands = (maps, measured, sampling, prior_image, y_table, z_table, w_first, w_middle, w_last)
    kernel = pl.pallas_call(
        functools.partial(step_kernel, shares, coils),
        out_shape=[pltpu.VMEM(brick, jnp.float32)] * 2,
        in_specs=[pl.BlockSpec(memory_space=pl.ANY)] * 9,
        out_specs=[pl.BlockSpec(memory_space=pltpu.VMEM)] * 2,
        scratch_shapes=[pltpu.VMEM(operand.shape, operand.dtype) for operand in operands]
        + [
            pltpu.SemaphoreType.DMA((len(operands),)),
            pltpu.VMEM((2,) + image, jnp.float32),
            pltpu.VMEM((4, planes, height, width), jnp.int32),
            pltpu.VMEM((4, coils - 1, planes, block, width), jnp.int32),
            pltpu.VMEM(brick, jnp.float32),
            pltpu.VMEM(image, jnp.float32),
            pltpu.VMEM(brick, jnp.float32),
            pltpu.VMEM((2, height, width), jnp.float32),
            pltpu.VMEM((2, 1, 128), jnp.float32),
            pltpu.VMEM((2, shares * coils - 1, 1, 128), jnp.float32),
            pltpu.VMEM((2, block + 2 * layers, 2 * planes, width), jnp.float32),
            pltpu.VMEM((2, deep, shares + 2, 2 * planes, width), jnp.float32),
            pltpu.VMEM((56, 128), jnp.float32),
            pltpu.VMEM((8 * channels, 256), jnp.bfloat16),
            pltpu.VMEM((layers - 2, 2 * y_outs * 3 * channels, (y_outs + 2) * 4 * channels), jnp.bfloat16),
            pltpu.VMEM((12 * tall, (rows + 2) * 4 * channels), jnp.bfloat16),
            pltpu.VMEM((deep, 80, whole // 8 * width), jnp.bfloat16),
            pltpu.VMEM(hidden, jnp.bfloat16),
            pltpu.VMEM(hidden, jnp.bfloat16),
            pltpu.VMEM((shares, 2 * planes, tall, width), jnp.float32),
            pltpu.VMEM((shares, 2 * planes, tall, width), jnp.float32),
            pltpu.SemaphoreType.DMA((4, planes, coils - 1)),
            pltpu.SemaphoreType.DMA((4, planes, coils - 1)),
            pltpu.SemaphoreType.DMA((2,)),
            pltpu.SemaphoreType.DMA((2,)),
            pltpu.SemaphoreType.DMA((2, 2)),
            pltpu.SemaphoreType.DMA((2, 2)),
            pltpu.SemaphoreType.DMA((2, shares - 1)),
            pltpu.SemaphoreType.DMA((2, shares - 1)),
            pltpu.SemaphoreType.DMA((shares - 1,)),
            pltpu.SemaphoreType.DMA((shares - 1,)),
        ],
        compiler_params=pltpu.CompilerParams(
            collective_id=0, has_side_effects=True, vmem_limit_bytes=56 * 1024 * 1024
        ),
    )
    half, correction = kernel(*operands)
    image = half + half
    return image, image + correction


def solution(mesh):
    placed = (
        P("coil", None, "slab", None, None),
        P("coil", None, "slab", None, None),
        P("slab", None, None),
        P(None, "slab", "coil", None),
        P(),
        P(),
        P(),
    )
    return jax.shard_map(
        body,
        mesh=mesh,
        in_specs=placed,
        out_specs=(P(None, "slab", "coil", None), P(None, "slab", "coil", None)),
        check_vma=False,
    )
```

```python
import functools

import jax
import jax.numpy as jnp
import numpy as np
from jax import lax
from jax.experimental import pallas as pl
from jax.experimental.pallas import tpu as pltpu
from jax.sharding import PartitionSpec as P

LAMBDA = 0.5
MESH = pl.DeviceIdType.MESH


def dft_parts(length):
    positions = np.arange(length)
    angles = 2.0 * np.pi / length * (positions[:, None] * positions[None, :] % length)
    return np.cos(angles) / np.sqrt(length), np.sin(angles) / np.sqrt(length)


def halves(table):
    table = table.astype(np.float32)
    high = table.astype(jnp.bfloat16)
    low = (table - high.astype(np.float32)).astype(jnp.bfloat16)
    return high, low


def split(values):
    high = values.astype(jnp.bfloat16)
    return high, (values - high.astype(jnp.float32)).astype(jnp.bfloat16)


def multiply(left, right):
    return jnp.dot(left, right, preferred_element_type=jnp.float32)


def transform(real, imag, y_table, z_table):
    rows, width = real.shape
    high, low = split(jnp.concatenate([real, imag], axis=1))
    y_high, y_low = y_table[:, :rows], y_table[:, rows:]
    z_high, z_low = z_table[: 2 * width], z_table[2 * width :]
    field = multiply(
        jnp.concatenate([y_high, y_high, y_low], axis=1), jnp.concatenate([high, low, high], axis=0)
    )
    field = jnp.concatenate(
        [field[:rows, :width] + field[rows:, width:], field[:rows, width:] - field[rows:, :width]], axis=1
    )
    high, low = split(field)
    field = multiply(
        jnp.concatenate([high, low, high], axis=1), jnp.concatenate([z_high, z_high, z_low], axis=0)
    )
    return field[:, :width], field[:, width:]


def fold(values):
    return jnp.sum(values.reshape(values.shape[0] // 8, 8, values.shape[1]), axis=0)


def total_of(values):
    return jnp.sum(jnp.sum(values, axis=0, keepdims=True), axis=1, keepdims=True)


BIAS = 128
LOW_HALF = 65535


def pack(real, imag):
    largest = jnp.maximum(
        jnp.max(jnp.abs(real), axis=0, keepdims=True), jnp.max(jnp.abs(imag), axis=0, keepdims=True)
    )
    exponent = jnp.maximum(jnp.ceil(jnp.log2(jnp.maximum(largest, 1e-35)) - 14.98), -110.0)
    scale = jnp.exp2(-exponent)
    real = jnp.round(real * scale).astype(jnp.int32)
    imag = jnp.round(imag * scale).astype(jnp.int32)
    code = exponent.astype(jnp.int32) + BIAS
    places = lax.broadcasted_iota(jnp.int32, (8, real.shape[1]), 0)
    bits = jnp.bitwise_and(jnp.right_shift(jnp.broadcast_to(code, places.shape), places), 1)
    head = jnp.bitwise_or(jnp.bitwise_and(real[:8], -2), bits)
    real = jnp.concatenate([head, real[8:]], axis=0)
    return jnp.bitwise_or(jnp.left_shift(real, 16), jnp.bitwise_and(imag, LOW_HALF))


def unpack(words):
    real = jnp.right_shift(words, 16)
    imag = jnp.right_shift(jnp.left_shift(words, 16), 16)
    places = lax.broadcasted_iota(jnp.int32, (8, words.shape[1]), 0)
    bits = jnp.left_shift(jnp.bitwise_and(real[:8], 1), places)
    code = jnp.sum(bits, axis=0, keepdims=True)
    scale = jnp.exp2((code - BIAS).astype(jnp.float32))
    return real.astype(jnp.float32) * scale, imag.astype(jnp.float32) * scale


def spread(blocks, x_out):
    empty = jnp.zeros_like(blocks[0])
    return jnp.concatenate([empty] * x_out + blocks + [empty] * (1 - x_out), axis=1)


def first_weights(taps, base, table, mirrored):
    outs = taps.shape[-1]
    for u in range(3):
        for v in range(3):
            for t in range(3):
                index = ((v * 3 + t) * 3 + u) * 2
                base[index : index + 2, :outs] = taps[u, jnp.where(mirrored, 2 - v, v), t].astype(jnp.float32)
    window = (24, table.shape[0])
    row = lax.broadcasted_iota(jnp.int32, window, 0)
    place = row - 2 * (lax.broadcasted_iota(jnp.int32, window, 1) // outs) - 2
    rest = jnp.zeros((8, window[1]), jnp.float32)
    blocks = []
    for v in range(3):
        for t in range(3):
            block = jnp.zeros(window, jnp.float32)
            for k in range(6):
                index = (v * 3 + t) * 6 + k
                line = jnp.concatenate([base[index : index + 1, :outs]] * (window[1] // outs), axis=1)
                block = jnp.where(place == k, line, block)
            blocks.append(block)
        blocks.append(rest)
    blocks.append(jnp.zeros((16, window[1]), jnp.float32))
    table[...] = jnp.transpose(jnp.concatenate(blocks, axis=0)).astype(table.dtype)


def middle_weights(taps, table, y_outs, mirrored):
    count, channels = taps.shape[3:]
    span = 4 * channels
    table[...] = jnp.zeros(table.shape, table.dtype)
    for layer in range(taps.shape[0]):
        for v in range(3):
            for x_out in range(2):
                block = spread([taps[layer, u, jnp.where(mirrored, 2 - v, v)] for u in range(3)], x_out)
                for y_out in range(y_outs):
                    base = (x_out * y_outs + y_out) * count
                    y_in = y_out + v
                    table[layer, base : base + count, y_in * span : (y_in + 1) * span] = block


def last_weights(taps, table, tall, mirrored):
    channels = taps.shape[-1]
    span = 4 * channels
    row = lax.broadcasted_iota(jnp.int32, (tall, span), 0)
    for t in range(3):
        for x_out in range(2):
            lines = [spread([taps[u, v, t].astype(jnp.float32) for u in range(3)], x_out) for v in range(3)]
            for o in range(2):
                base = ((t * 2 + x_out) * 2 + o) * tall
                count = table.shape[1] // span
                for index in range(count):
                    y_in = jnp.where(mirrored, count - 1 - index, index)
                    block = jnp.zeros((tall, span), jnp.float32)
                    for v in range(3):
                        block = jnp.where(row == y_in - v, lines[v][o : o + 1], block)
                    table[base : base + tall, index * span : (index + 1) * span] = block.astype(table.dtype)


def along_z(before, centre, after, lanes):
    width = centre.shape[1]
    before = jnp.where(lanes == 0, 0.0, pltpu.roll(before, 1, 1))
    after = jnp.where(lanes == width - 1, 0.0, pltpu.roll(after, width - 1, 1))
    return centre + before + after


def conv_first(table, taken, sink, rows, inside, ready):
    outs = sink.shape[2]
    width = sink.shape[3]
    depth = 3 * taken.shape[1]
    for y in range(rows):
        product = multiply(table[:, :depth], taken[y : y + 3].reshape(depth, taken.shape[2]))
        for group in range(taken.shape[2] // width):
            for q in range(table.shape[0] // outs):
                value = product[q * outs : (q + 1) * outs, group * width : (group + 1) * width]
                value = jnp.where(inside(y), jnp.maximum(value, 0.0), 0.0)
                sink[y + 1, group * (table.shape[0] // outs) + q + 1] = value.astype(jnp.bfloat16)
        if y == 0:
            ready()


def conv_middle(table, source, sink, rows, y_outs, inside, ready):
    planes, outs, width = source.shape[1] - 2, source.shape[2], source.shape[3]
    lanes = lax.broadcasted_iota(jnp.int32, (outs, width), 1)
    group = 2 if planes % 4 == 0 else 1
    for y in range(0, rows, y_outs):
        tall = min(y_outs, rows - y)
        depth = (tall + 2) * 4 * outs
        if tall == y_outs:
            weights = table[...]
        else:
            step = 3 * outs
            weights = [table[x * y_outs * step : (x * y_outs + tall) * step, :depth] for x in range(2)]
            weights = jnp.concatenate(weights, axis=0)
        for first in range(0, planes, 2 * group):
            taken = [
                source[y : y + tall + 2, first + 2 * k : first + 2 * k + 4].reshape(depth, width)
                for k in range(group)
            ]
            product = multiply(weights, jnp.concatenate(taken, axis=1))
            for x_out in range(2):
                for y_out in range(tall):
                    base = (x_out * tall + y_out) * 3 * outs
                    for k in range(group):
                        parts = [
                            product[base + t * outs : base + (t + 1) * outs, k * width : (k + 1) * width]
                            for t in range(3)
                        ]
                        value = along_z(*parts, lanes)
                        value = jnp.where(inside(y + y_out), jnp.maximum(value, 0.0), 0.0)
                        sink[y + y_out + 1, first + 2 * k + x_out + 1] = value.astype(jnp.bfloat16)
        if y == 0:
            ready()


def conv_last(table, source, sink, rows, order, ready):
    channels, width = source.shape[2], source.shape[3]
    tall = table.shape[0] // 3
    lanes = lax.broadcasted_iota(jnp.int32, (tall, width), 1)
    depth = (rows + 2) * 4 * channels
    for first in range(0, len(order), 2):
        targets = order[first : first + 2]
        taken = [source[: rows + 2, pl.ds(2 * target, 4)].reshape(depth, width) for target in targets]
        product = multiply(table[...], jnp.concatenate(taken, axis=1))
        for k, target in enumerate(targets):
            parts = [product[t * tall : (t + 1) * tall, k * width : (k + 1) * width] for t in range(3)]
            sink[target] = along_z(*parts, lanes).reshape(sink.shape[1:])
        for k, target in enumerate(targets):
            ready(first + k, target)


def step_kernel(
    shares, coils, *refs,
):
    outside, (half, correction), refs = refs[:9], refs[9:11], refs[11:]
    inside, load_sem, refs = refs[:9], refs[9], refs[10:]
    maps, measured, mask, prior, y_table, z_table, w_first, w_middle, w_last = inside
    (
        part, outbox, inbox, own_rhs, rhs, own_image, residual, note, notes, fields, taken_fields,
        base, first_table, middle_table, last_table, shifted, corrections, arrived,
        block_send, block_recv, note_send, note_recv, edge_send, edge_recv, field_send, field_recv, back_send, back_recv,
        pair_send, pair_recv, *hidden,
    ) = refs
    loads = [
        pltpu.make_async_copy(source, target, load_sem.at[index])
        for index, (source, target) in enumerate(zip(outside, inside))
    ]
    for index in (1, 2, 4, 5, 0, 6, 8, 3, 7):
        loads[index].start()
    slab = lax.axis_index("slab")
    coil = lax.axis_index("coil")
    devices = shares * coils
    planes = maps.shape[1]
    height, width = maps.shape[2:]
    block = prior.shape[2]
    rows = block // shares
    layers = w_middle.shape[0] + 2
    halo = layers
    y_outs = 2 if rows % 2 == 0 else 1
    tables = (y_table, z_table)

    offsets = [(s, c) for s in range(shares) for c in range(coils) if s or c]
    offsets.sort(key=lambda offset: -min(offset[1], coils - offset[1]) - bin(offset[0] // 2).count("1"))

    def device_at(distance):
        far_slab, far_coil = offsets[distance - 1]
        return (lax.rem(slab + far_slab, shares), lax.rem(coil + far_coil, coils))

    barrier = pltpu.get_barrier_semaphore()
    for distance in range(1, devices):
        pl.semaphore_signal(barrier, inc=1, device_id=device_at(distance), device_id_type=MESH)

    def rows_of(index):
        return pl.ds(pl.multiple_of(index * block, block), block)

    mine = rows_of(coil)

    def send(source, target, send_sem, recv_sem, device):
        copy = pltpu.make_async_remote_copy(
            src_ref=source, dst_ref=target, send_sem=send_sem, recv_sem=recv_sem,
            device_id=device, device_id_type=MESH,
        )
        copy.start()
        return copy

    def to_coils(phase, p, source, target):
        copies = []
        for distance in range(1, coils):
            other = lax.rem(coil + distance, coils)
            copies.append(
                send(
                    source(other), target(distance), block_send.at[phase, p, distance - 1],
                    block_recv.at[phase, p, distance - 1], (slab, other),
                )
            )
        return copies

    def scatter(phase, p):
        return to_coils(
            phase, p, lambda other: outbox.at[phase, p, rows_of(other)],
            lambda distance: inbox.at[phase, distance - 1, p],
        )

    def gather(phase, p):
        return to_coils(
            phase, p, lambda other: outbox.at[phase, p, pl.ds(0, block)],
            lambda distance: inbox.at[phase, distance - 1, p],
        )

    def tell(phase):
        for distance in range(1, devices):
            send(
                note.at[phase], notes.at[phase, distance - 1], note_send.at[phase], note_recv.at[phase],
                device_at(distance),
            )
        return pltpu.make_async_remote_copy(
            src_ref=notes.at[phase], dst_ref=notes.at[phase], send_sem=note_send.at[phase],
            recv_sem=note_recv.at[phase], device_id=device_at(1), device_id_type=MESH,
        )

    def send_edges(which):
        above = lax.rem(coil + coils - 1, coils)
        below = lax.rem(coil + 1, coils)
        ends = ((block, 0, below), (halo, halo + block, above))
        return [
            send(
                fields.at[which, pl.ds(source, halo)], fields.at[which, pl.ds(target, halo)],
                edge_send.at[which, side], edge_recv.at[which, side], (slab, other),
            )
            for side, (source, target, other) in enumerate(ends)
        ]

    deep = rows + 2 * halo

    def send_fields(which, copies):
        finish(copies)
        top_edge = fields[which, :halo]
        fields[which, :halo] = jnp.where(coil > 0, top_edge, 0.0)
        low_edge = fields[which, halo + block :]
        fields[which, halo + block :] = jnp.where(coil < coils - 1, low_edge, 0.0)
        copies = []
        for distance in range(1, shares):
            other = lax.rem(slab + distance, shares)
            copies.append(
                send(
                    fields.at[which, pl.ds(other * rows, deep)], taken_fields.at[which, :, slab + 1],
                    field_send.at[which, distance - 1], field_recv.at[which, distance - 1], (other, coil),
                )
            )
        taken_fields[which, :, slab + 1] = fields[which, pl.ds(slab * rows, deep)]
        return copies

    sent = []

    def finish(copies):
        for copy in copies:
            copy.wait_recv()
        sent.extend(copies)

    lanes = lax.broadcasted_iota(jnp.int32, (1, note.shape[2]), 1)

    def write_note(phase, values):
        line = jnp.zeros(lanes.shape, jnp.float32)
        for index, value in enumerate(values):
            line = jnp.where(lanes == index, value, line)
        note[phase] = line

    def read_notes(phase, count):
        line = note[phase]
        for distance in range(1, devices):
            line = line + notes[phase, distance - 1]
        return [jnp.sum(jnp.where(lanes == index, line, 0.0), axis=1, keepdims=True) for index in range(count)]

    def backward_part(real, imag, phase, p):
        imag, real = transform(imag, real, *tables)
        part_re = maps[0, p] * real + maps[1, p] * imag
        part_im = maps[0, p] * imag - maps[1, p] * real
        part[phase, 0, p] = part_re
        part[phase, 1, p] = part_im
        for index in range(coils):
            span = slice(index * block, (index + 1) * block)
            outbox[phase, p, span] = pack(part_re[span], part_im[span])

    def forward(image_re, image_im, p):
        real = maps[0, p] * image_re - maps[1, p] * image_im
        imag = maps[0, p] * image_im + maps[1, p] * image_re
        real, imag = transform(real, imag, *tables)
        sampled = mask[p].astype(jnp.float32)
        return real * sampled, imag * sampled

    def reduced(phase, p):
        real = part[phase, 0, p, mine]
        imag = part[phase, 1, p, mine]
        for distance in range(1, coils):
            more = unpack(inbox[phase, distance - 1, p])
            real = real + more[0]
            imag = imag + more[1]
        return real, imag

    pending = []
    for index in (1, 2, 4, 5, 0):
        loads[index].wait()
    for p in range(planes):
        sampled = mask[p].astype(jnp.float32)
        backward_part(measured[0, p] * sampled, measured[1, p] * sampled, 0, p)
        if p == 0:
            pl.semaphore_wait(barrier, devices - 1)
        pending.append(scatter(0, p))
    for index in (6, 8, 3, 7):
        loads[index].wait()
    mirrored = lax.rem(slab, 2) == 0
    first_weights(w_first, base, first_table, mirrored)
    last_weights(w_last, last_table, last_table.shape[0] // 12, mirrored)
    total = taken_fields.shape[2]
    for which in range(2):
        for outer in (0, total - 1):
            taken_fields[which, :, outer] = jnp.zeros((deep,) + taken_fields.shape[3:], jnp.float32)
    shifted[...] = jnp.zeros(shifted.shape, shifted.dtype)
    for buffer in hidden:
        for outer in (0, buffer.shape[1] - 1):
            buffer[:, outer] = jnp.zeros((buffer.shape[0],) + buffer.shape[2:], buffer.dtype)
    gathers = []
    norm = jnp.zeros((8, width), jnp.float32)
    for p in range(planes):
        finish(pending[p])
        real, imag = reduced(0, p)
        real = real + LAMBDA * prior[0, p]
        imag = imag + LAMBDA * prior[1, p]
        outbox[2, p, :block] = pack(real, imag)
        gathers.append(gather(2, p))
        for h, value in enumerate((real, imag)):
            own_rhs[h, p] = value
            rhs[h, p, mine] = value
            fields[0, halo : halo + block, 2 * p + h] = value
            norm = norm + fold(value * value)
    edge_copies = send_edges(0)
    middle_weights(w_middle, middle_table, y_outs, mirrored)
    energy = LAMBDA * norm
    pending = []
    for p in range(planes):
        finish(gathers[p])
        for distance in range(1, coils):
            source = rows_of(lax.rem(coil + coils - distance, coils))
            real, imag = unpack(inbox[2, distance - 1, p])
            rhs[0, p, source] = real
            rhs[1, p, source] = imag
        real, imag = forward(rhs[0, p], rhs[1, p], p)
        energy = energy + fold(real * real + imag * imag)
        backward_part(real, imag, 1, p)
        pending.append(scatter(1, p))
    write_note(0, [total_of(norm), total_of(energy)])
    first_notes = tell(0)
    field_copies = send_fields(0, edge_copies)
    gathers = []
    for p in range(planes):
        finish(pending[p])
        images = reduced(1, p)
        images = [images[h] + LAMBDA * own_rhs[h, p] for h in range(2)]
        outbox[3, p, :block] = pack(*images)
        if p < planes - 1:
            gathers.append(gather(3, p))
        for h in range(2):
            own_image[h, p] = images[h]
            fields[1, halo : halo + block, 2 * p + h] = images[h]
    edge_copies = send_edges(1)
    gathers.append(gather(3, planes - 1))
    first_notes.wait_recv()
    norm, curvature = read_notes(0, 2)
    step = norm / curvature
    norm_next = jnp.zeros((8, width), jnp.float32)
    cross = jnp.zeros((8, width), jnp.float32)
    for p in range(planes):
        for h in range(2):
            image = own_image[h, p]
            value = own_rhs[h, p] - step * image
            norm_next = norm_next + fold(value * value)
            cross = cross + fold(value * image)
    energy = LAMBDA * norm_next
    norm_next, cross = total_of(norm_next), total_of(cross)
    for p in range(planes):
        finish(gathers[p])
        for h in range(2):
            residual[h, mine] = own_rhs[h, p] - step * own_image[h, p]
        for distance in range(1, coils):
            source = rows_of(lax.rem(coil + coils - distance, coils))
            for h, value in enumerate(unpack(inbox[3, distance - 1, p])):
                residual[h, source] = rhs[h, p, source] - step * value
        real, imag = forward(residual[0], residual[1], p)
        energy = energy + fold(real * real + imag * imag)
        if p == 0:
            field_copies = field_copies + send_fields(1, edge_copies)
    write_note(1, [norm_next, total_of(energy), cross])
    last_notes = tell(1)
    finish(field_copies)
    last_notes.wait_recv()
    norm_next, energy, cross = read_notes(1, 3)
    ratio = norm_next / norm
    curvature = energy + 2.0 * ratio * cross + ratio * ratio * curvature
    step_next = norm_next / curvature
    share = step + step_next * (1.0 + ratio)
    share_image = -step_next * step
    across = lax.broadcasted_iota(jnp.int32, (4 * total, width), 1)
    for index in range(shifted.shape[0]):
        y = jnp.where(mirrored, rows + halo - index, halo - 1 + index)
        line = share * taken_fields[0, y].reshape(4 * total, width)
        line = line + share_image * taken_fields[1, y].reshape(4 * total, width)
        line = line.astype(jnp.bfloat16).astype(jnp.float32)
        before = jnp.where(across == 0, 0.0, pltpu.roll(line, 1, 1))
        after = jnp.where(across == width - 1, 0.0, pltpu.roll(line, width - 1, 1))
        for group in range(shifted.shape[2] // width):
            span = slice(16 * group, 16 * group + 24)
            piece = jnp.concatenate([before[span], line[span], after[span], jnp.zeros((8, width), jnp.float32)], axis=0)
            shifted[index, :, group * width : (group + 1) * width] = piece.astype(jnp.bfloat16)
    for h in range(2):
        for p in range(planes):
            half[h, p] = 0.5 * (share * own_rhs[h, p] + share_image * own_image[h, p])
    top = coil * block + slab * rows
    partner = slab + 1 - 2 * lax.rem(slab, 2)
    exchanged = []

    def inside(m):
        y = top + jnp.where(mirrored, rows - 1 - m, m)
        return jnp.logical_and(y >= 0, y < height)

    def share_row(layer):
        buffer = hidden[layer]
        exchanged.append(
            send(buffer.at[1], buffer.at[0], pair_send.at[layer], pair_recv.at[layer], (partner, coil))
        )

    conv_first(first_table, shifted, hidden[0], rows + layers - 1, inside, lambda: share_row(0))
    for layer in range(layers - 2):
        finish(exchanged[-1:])
        conv_middle(
            middle_table.at[layer], hidden[layer], hidden[layer + 1], rows + layers - 2 - layer, y_outs, inside,
            lambda: share_row(layer + 1),
        )
    finish(exchanged[-1:])
    copies = []

    def give(index, other):
        if index < shares - 1:
            copies.append(
                send(
                    corrections.at[other], arrived.at[slab], back_send.at[index], back_recv.at[index], (other, coil)
                )
            )

    order = [lax.rem(slab + shares - 1 - index, shares) for index in range(shares)]
    conv_last(last_table, hidden[layers - 2], corrections, rows, order, give)
    arrived[slab] = corrections[slab]
    for copy in sent:
        copy.wait_send()
    first_notes.wait_send()
    last_notes.wait_send()
    sent.clear()
    finish(copies)
    for copy in copies:
        copy.wait_send()
    for s in range(shares):
        span = slice(s * rows, (s + 1) * rows)
        for p in range(planes):
            for h in range(2):
                correction[h, p, span] = arrived[s, 2 * p + h, :rows]


def body(sensitivity, kspace, sampling, prior_image, w_first, w_middle, w_last):
    maps, measured = sensitivity[0], kspace[0]
    planes, height, width = sampling.shape
    block = prior_image.shape[2]
    shares = lax.axis_size("slab")
    coils = lax.axis_size("coil")
    rows = block // shares
    channels = w_first.shape[0]
    layers = w_middle.shape[0] + 2
    whole = shares * planes
    y_outs = 2 if rows % 2 == 0 else 1
    cosine, sine = dft_parts(height)
    high, low = halves(np.concatenate([cosine, sine]))
    y_table = np.concatenate([high, low], axis=1)
    cosine, sine = dft_parts(width)
    high, low = halves(np.block([[cosine, -sine], [sine, cosine]]))
    z_table = np.concatenate([high, low], axis=0)
    w_first = jnp.transpose(w_first, (2, 3, 4, 1, 0))
    w_middle = jnp.transpose(w_middle, (0, 3, 4, 5, 1, 2)).reshape(layers - 2, 3, 3, 3 * channels, channels)
    w_last = jnp.transpose(w_last, (2, 3, 4, 0, 1))
    image = (2, planes, height, width)
    brick = (2, planes, block, width)
    tall = rows + -rows % 8
    deep = rows + 2 * layers
    operands = (maps, measured, sampling, prior_image, y_table, z_table, w_first, w_middle, w_last)
    kernel = pl.pallas_call(
        functools.partial(step_kernel, shares, coils),
        out_shape=[pltpu.VMEM(brick, jnp.float32)] * 2,
        in_specs=[pl.BlockSpec(memory_space=pl.ANY)] * 9,
        out_specs=[pl.BlockSpec(memory_space=pltpu.VMEM)] * 2,
        scratch_shapes=[pltpu.VMEM(operand.shape, operand.dtype) for operand in operands]
        + [
            pltpu.SemaphoreType.DMA((len(operands),)),
            pltpu.VMEM((2,) + image, jnp.float32),
            pltpu.VMEM((4, planes, height, width), jnp.int32),
            pltpu.VMEM((4, coils - 1, planes, block, width), jnp.int32),
            pltpu.VMEM(brick, jnp.float32),
            pltpu.VMEM(image, jnp.float32),
            pltpu.VMEM(brick, jnp.float32),
            pltpu.VMEM((2, height, width), jnp.float32),
            pltpu.VMEM((2, 1, 128), jnp.float32),
            pltpu.VMEM((2, shares * coils - 1, 1, 128), jnp.float32),
            pltpu.VMEM((2, block + 2 * layers, 2 * planes, width), jnp.float32),
            pltpu.VMEM((2, deep, shares + 2, 2 * planes, width), jnp.float32),
            pltpu.VMEM((56, 128), jnp.float32),
            pltpu.VMEM((8 * channels, 256), jnp.bfloat16),
            pltpu.VMEM((layers - 2, 2 * y_outs * 3 * channels, (y_outs + 2) * 4 * channels), jnp.bfloat16),
            pltpu.VMEM((12 * tall, (rows + 2) * 4 * channels), jnp.bfloat16),
            pltpu.VMEM((rows + layers + 1, 80, whole // 8 * width), jnp.bfloat16),
            pltpu.VMEM((shares, 2 * planes, tall, width), jnp.float32),
            pltpu.VMEM((shares, 2 * planes, tall, width), jnp.float32),
            pltpu.SemaphoreType.DMA((4, planes, coils - 1)),
            pltpu.SemaphoreType.DMA((4, planes, coils - 1)),
            pltpu.SemaphoreType.DMA((2,)),
            pltpu.SemaphoreType.DMA((2,)),
            pltpu.SemaphoreType.DMA((2, 2)),
            pltpu.SemaphoreType.DMA((2, 2)),
            pltpu.SemaphoreType.DMA((2, shares - 1)),
            pltpu.SemaphoreType.DMA((2, shares - 1)),
            pltpu.SemaphoreType.DMA((shares - 1,)),
            pltpu.SemaphoreType.DMA((shares - 1,)),
            pltpu.SemaphoreType.DMA((layers - 1,)),
            pltpu.SemaphoreType.DMA((layers - 1,)),
        ]
        + [
            pltpu.VMEM((rows + layers - layer, whole + 2, channels, width), jnp.bfloat16)
            for layer in range(layers - 1)
        ],
        compiler_params=pltpu.CompilerParams(
            collective_id=0, has_side_effects=True, vmem_limit_bytes=56 * 1024 * 1024
        ),
    )
    half, correction = kernel(*operands)
    image = half + half
    return image, image + correction


def solution(mesh):
    placed = (
        P("coil", None, "slab", None, None),
        P("coil", None, "slab", None, None),
        P("slab", None, None),
        P(None, "slab", "coil", None),
        P(),
        P(),
        P(),
    )
    return jax.shard_map(
        body,
        mesh=mesh,
        in_specs=placed,
        out_specs=(P(None, "slab", "coil", None), P(None, "slab", "coil", None)),
        check_vma=False,
    )
```

```python
import functools

import jax
import jax.numpy as jnp
import numpy as np
from jax import lax
from jax.experimental import pallas as pl
from jax.experimental.pallas import tpu as pltpu
from jax.sharding import PartitionSpec as P

LAMBDA = 0.5
MESH = pl.DeviceIdType.MESH


def dft_parts(length):
    positions = np.arange(length)
    angles = 2.0 * np.pi / length * (positions[:, None] * positions[None, :] % length)
    return np.cos(angles) / np.sqrt(length), np.sin(angles) / np.sqrt(length)


def halves(table):
    table = table.astype(np.float32)
    high = table.astype(jnp.bfloat16)
    low = (table - high.astype(np.float32)).astype(jnp.bfloat16)
    return high, low


def split(values):
    high = values.astype(jnp.bfloat16)
    return high, (values - high.astype(jnp.float32)).astype(jnp.bfloat16)


def multiply(left, right):
    return jnp.dot(left, right, preferred_element_type=jnp.float32)


def transform(real, imag, y_table, z_table):
    rows, width = real.shape
    high, low = split(jnp.concatenate([real, imag], axis=1))
    y_high, y_low = y_table[:, :rows], y_table[:, rows:]
    z_high, z_low = z_table[: 2 * width], z_table[2 * width :]
    field = multiply(
        jnp.concatenate([y_high, y_high, y_low], axis=1), jnp.concatenate([high, low, high], axis=0)
    )
    field = jnp.concatenate(
        [field[:rows, :width] + field[rows:, width:], field[:rows, width:] - field[rows:, :width]], axis=1
    )
    high, low = split(field)
    field = multiply(
        jnp.concatenate([high, low, high], axis=1), jnp.concatenate([z_high, z_high, z_low], axis=0)
    )
    return field[:, :width], field[:, width:]


def fold(values):
    return jnp.sum(values.reshape(values.shape[0] // 8, 8, values.shape[1]), axis=0)


def total_of(values):
    return jnp.sum(jnp.sum(values, axis=0, keepdims=True), axis=1, keepdims=True)


BIAS = 128
LOW_HALF = 65535


def pack(real, imag):
    largest = jnp.maximum(
        jnp.max(jnp.abs(real), axis=0, keepdims=True), jnp.max(jnp.abs(imag), axis=0, keepdims=True)
    )
    exponent = jnp.maximum(jnp.ceil(jnp.log2(jnp.maximum(largest, 1e-35)) - 14.98), -110.0)
    scale = jnp.exp2(-exponent)
    real = jnp.round(real * scale).astype(jnp.int32)
    imag = jnp.round(imag * scale).astype(jnp.int32)
    code = exponent.astype(jnp.int32) + BIAS
    places = lax.broadcasted_iota(jnp.int32, (8, real.shape[1]), 0)
    bits = jnp.bitwise_and(jnp.right_shift(jnp.broadcast_to(code, places.shape), places), 1)
    head = jnp.bitwise_or(jnp.bitwise_and(real[:8], -2), bits)
    real = jnp.concatenate([head, real[8:]], axis=0)
    return jnp.bitwise_or(jnp.left_shift(real, 16), jnp.bitwise_and(imag, LOW_HALF))


def unpack(words):
    real = jnp.right_shift(words, 16)
    imag = jnp.right_shift(jnp.left_shift(words, 16), 16)
    places = lax.broadcasted_iota(jnp.int32, (8, words.shape[1]), 0)
    bits = jnp.left_shift(jnp.bitwise_and(real[:8], 1), places)
    code = jnp.sum(bits, axis=0, keepdims=True)
    scale = jnp.exp2((code - BIAS).astype(jnp.float32))
    return real.astype(jnp.float32) * scale, imag.astype(jnp.float32) * scale


def spread(blocks, x_out):
    empty = jnp.zeros_like(blocks[0])
    return jnp.concatenate([empty] * x_out + blocks + [empty] * (1 - x_out), axis=1)


def first_weights(taps, base, table):
    outs = taps.shape[-1]
    for u in range(3):
        for v in range(3):
            for t in range(3):
                index = ((v * 3 + t) * 3 + u) * 2
                base[index : index + 2, :outs] = taps[u, v, t].astype(jnp.float32)
    window = (24, table.shape[0])
    row = lax.broadcasted_iota(jnp.int32, window, 0)
    place = row - 2 * (lax.broadcasted_iota(jnp.int32, window, 1) // outs) - 2
    rest = jnp.zeros((8, window[1]), jnp.float32)
    blocks = []
    for v in range(3):
        for t in range(3):
            block = jnp.zeros(window, jnp.float32)
            for k in range(6):
                index = (v * 3 + t) * 6 + k
                line = jnp.concatenate([base[index : index + 1, :outs]] * (window[1] // outs), axis=1)
                block = jnp.where(place == k, line, block)
            blocks.append(block)
        blocks.append(rest)
    blocks.append(jnp.zeros((16, window[1]), jnp.float32))
    table[...] = jnp.transpose(jnp.concatenate(blocks, axis=0)).astype(table.dtype)


def middle_weights(taps, table, y_outs):
    count, channels = taps.shape[3:]
    span = 4 * channels
    table[...] = jnp.zeros(table.shape, table.dtype)
    for layer in range(taps.shape[0]):
        for v in range(3):
            for x_out in range(2):
                block = spread([taps[layer, u, v] for u in range(3)], x_out)
                for y_out in range(y_outs):
                    base = (x_out * y_outs + y_out) * count
                    y_in = y_out + v
                    table[layer, base : base + count, y_in * span : (y_in + 1) * span] = block


def last_weights(taps, table, tall):
    channels = taps.shape[-1]
    span = 4 * channels
    row = lax.broadcasted_iota(jnp.int32, (tall, span), 0)
    for t in range(3):
        for x_out in range(2):
            lines = [spread([taps[u, v, t].astype(jnp.float32) for u in range(3)], x_out) for v in range(3)]
            for o in range(2):
                base = ((t * 2 + x_out) * 2 + o) * tall
                for y_in in range(table.shape[1] // span):
                    block = jnp.zeros((tall, span), jnp.float32)
                    for v in range(3):
                        block = jnp.where(row == y_in - v, lines[v][o : o + 1], block)
                    table[base : base + tall, y_in * span : (y_in + 1) * span] = block.astype(table.dtype)


def along_z(before, centre, after, lanes):
    width = centre.shape[1]
    before = jnp.where(lanes == 0, 0.0, pltpu.roll(before, 1, 1))
    after = jnp.where(lanes == width - 1, 0.0, pltpu.roll(after, width - 1, 1))
    return centre + before + after


def conv_first(table, taken, sink, rows, top, height):
    outs = sink.shape[2]
    width = sink.shape[3]
    depth = 3 * taken.shape[1]
    for y in range(rows):
        inside = jnp.logical_and(top + y >= 0, top + y < height)
        product = multiply(table[:, :depth], taken[y : y + 3].reshape(depth, taken.shape[2]))
        for group in range(taken.shape[2] // width):
            for q in range(table.shape[0] // outs):
                value = product[q * outs : (q + 1) * outs, group * width : (group + 1) * width]
                value = jnp.where(inside, jnp.maximum(value, 0.0), 0.0)
                sink[y, group * (table.shape[0] // outs) + q + 1] = value.astype(jnp.bfloat16)


def conv_middle(table, source, sink, rows, y_outs, top, height):
    planes, outs, width = source.shape[1] - 2, source.shape[2], source.shape[3]
    lanes = lax.broadcasted_iota(jnp.int32, (outs, width), 1)
    depth = (y_outs + 2) * 4 * outs
    group = 2 if planes % 4 == 0 else 1
    for y in range(0, rows, y_outs):
        for first in range(0, planes, 2 * group):
            taken = [
                source[y : y + y_outs + 2, first + 2 * k : first + 2 * k + 4].reshape(depth, width)
                for k in range(group)
            ]
            product = multiply(table[...], jnp.concatenate(taken, axis=1))
            for x_out in range(2):
                for y_out in range(y_outs):
                    base = (x_out * y_outs + y_out) * 3 * outs
                    inside = jnp.logical_and(top + y + y_out >= 0, top + y + y_out < height)
                    for k in range(group):
                        parts = [
                            product[base + t * outs : base + (t + 1) * outs, k * width : (k + 1) * width]
                            for t in range(3)
                        ]
                        value = along_z(*parts, lanes)
                        value = jnp.where(inside, jnp.maximum(value, 0.0), 0.0)
                        sink[y + y_out, first + 2 * k + x_out + 1] = value.astype(jnp.bfloat16)


def conv_last(table, source, sink, rows, order, ready):
    channels, width = source.shape[2], source.shape[3]
    tall = table.shape[0] // 3
    lanes = lax.broadcasted_iota(jnp.int32, (tall, width), 1)
    depth = (rows + 2) * 4 * channels
    for first in range(0, len(order), 2):
        targets = order[first : first + 2]
        taken = [source[: rows + 2, pl.ds(2 * target, 4)].reshape(depth, width) for target in targets]
        product = multiply(table[...], jnp.concatenate(taken, axis=1))
        for k, target in enumerate(targets):
            parts = [product[t * tall : (t + 1) * tall, k * width : (k + 1) * width] for t in range(3)]
            sink[target] = along_z(*parts, lanes).reshape(sink.shape[1:])
        for k, target in enumerate(targets):
            ready(first + k, target)


def step_kernel(
    shares, coils, *refs,
):
    outside, (half, correction), refs = refs[:9], refs[9:11], refs[11:]
    inside, load_sem, refs = refs[:9], refs[9], refs[10:]
    maps, measured, mask, prior, y_table, z_table, w_first, w_middle, w_last = inside
    (
        part, outbox, inbox, own_rhs, rhs, own_image, residual, note, notes, fields, taken_fields,
        base, first_table, middle_table, last_table, shifted, even, odd, corrections, arrived,
        block_send, block_recv, note_send, note_recv, edge_send, edge_recv, field_send, field_recv, back_send, back_recv,
    ) = refs
    loads = [
        pltpu.make_async_copy(source, target, load_sem.at[index])
        for index, (source, target) in enumerate(zip(outside, inside))
    ]
    slab = lax.axis_index("slab")
    coil = lax.axis_index("coil")
    devices = shares * coils
    planes = maps.shape[1]
    height, width = maps.shape[2:]
    block = prior.shape[2]
    rows = block // shares
    layers = w_middle.shape[0] + 2
    halo = layers
    y_outs = 2 if rows % 2 == 0 else 1
    tables = (y_table, z_table)

    offsets = [(s, c) for s in range(shares) for c in range(coils) if s or c]
    offsets.sort(key=lambda offset: -min(offset[1], coils - offset[1]) - bin(offset[0] // 2).count("1"))

    def device_at(distance):
        far_slab, far_coil = offsets[distance - 1]
        return (lax.rem(slab + far_slab, shares), lax.rem(coil + far_coil, coils))

    barrier = pltpu.get_barrier_semaphore()
    for distance in range(1, devices):
        pl.semaphore_signal(barrier, inc=1, device_id=device_at(distance), device_id_type=MESH)

    for index in (1, 2, 4, 5, 0, 6, 8, 3, 7):
        loads[index].start()

    def rows_of(index):
        return pl.ds(pl.multiple_of(index * block, block), block)

    mine = rows_of(coil)

    def send(source, target, send_sem, recv_sem, device):
        copy = pltpu.make_async_remote_copy(
            src_ref=source, dst_ref=target, send_sem=send_sem, recv_sem=recv_sem,
            device_id=device, device_id_type=MESH,
        )
        copy.start()
        return copy

    def to_coils(phase, p, source, target):
        copies = []
        for distance in range(1, coils):
            other = lax.rem(coil + distance, coils)
            copies.append(
                send(
                    source(other), target(distance), block_send.at[phase, p, distance - 1],
                    block_recv.at[phase, p, distance - 1], (slab, other),
                )
            )
        return copies

    def scatter(phase, p):
        return to_coils(
            phase, p, lambda other: outbox.at[phase, p, rows_of(other)],
            lambda distance: inbox.at[phase, distance - 1, p],
        )

    def gather(phase, p):
        return to_coils(
            phase, p, lambda other: outbox.at[phase, p, pl.ds(0, block)],
            lambda distance: inbox.at[phase, distance - 1, p],
        )

    def tell(phase):
        for distance in range(1, devices):
            send(
                note.at[phase], notes.at[phase, distance - 1], note_send.at[phase], note_recv.at[phase],
                device_at(distance),
            )
        return pltpu.make_async_remote_copy(
            src_ref=notes.at[phase], dst_ref=notes.at[phase], send_sem=note_send.at[phase],
            recv_sem=note_recv.at[phase], device_id=device_at(1), device_id_type=MESH,
        )

    def send_edges(which):
        above = lax.rem(coil + coils - 1, coils)
        below = lax.rem(coil + 1, coils)
        ends = ((block, 0, below), (halo, halo + block, above))
        return [
            send(
                fields.at[which, pl.ds(source, halo)], fields.at[which, pl.ds(target, halo)],
                edge_send.at[which, side], edge_recv.at[which, side], (slab, other),
            )
            for side, (source, target, other) in enumerate(ends)
        ]

    deep = rows + 2 * halo

    def send_fields(which, copies):
        finish(copies)
        top_edge = fields[which, :halo]
        fields[which, :halo] = jnp.where(coil > 0, top_edge, 0.0)
        low_edge = fields[which, halo + block :]
        fields[which, halo + block :] = jnp.where(coil < coils - 1, low_edge, 0.0)
        copies = []
        for distance in range(1, shares):
            other = lax.rem(slab + distance, shares)
            copies.append(
                send(
                    fields.at[which, pl.ds(other * rows, deep)], taken_fields.at[which, :, slab + 1],
                    field_send.at[which, distance - 1], field_recv.at[which, distance - 1], (other, coil),
                )
            )
        taken_fields[which, :, slab + 1] = fields[which, pl.ds(slab * rows, deep)]
        return copies

    sent = []

    def finish(copies):
        for copy in copies:
            copy.wait_recv()
        sent.extend(copies)

    lanes = lax.broadcasted_iota(jnp.int32, (1, note.shape[2]), 1)

    def write_note(phase, values):
        line = jnp.zeros(lanes.shape, jnp.float32)
        for index, value in enumerate(values):
            line = jnp.where(lanes == index, value, line)
        note[phase] = line

    def read_notes(phase, count):
        line = note[phase]
        for distance in range(1, devices):
            line = line + notes[phase, distance - 1]
        return [jnp.sum(jnp.where(lanes == index, line, 0.0), axis=1, keepdims=True) for index in range(count)]

    def backward_part(real, imag, phase, p):
        imag, real = transform(imag, real, *tables)
        part_re = maps[0, p] * real + maps[1, p] * imag
        part_im = maps[0, p] * imag - maps[1, p] * real
        part[phase, 0, p] = part_re
        part[phase, 1, p] = part_im
        for index in range(coils):
            span = slice(index * block, (index + 1) * block)
            outbox[phase, p, span] = pack(part_re[span], part_im[span])

    def forward(image_re, image_im, p):
        real = maps[0, p] * image_re - maps[1, p] * image_im
        imag = maps[0, p] * image_im + maps[1, p] * image_re
        real, imag = transform(real, imag, *tables)
        sampled = mask[p].astype(jnp.float32)
        return real * sampled, imag * sampled

    def reduced(phase, p):
        real = part[phase, 0, p, mine]
        imag = part[phase, 1, p, mine]
        for distance in range(1, coils):
            more = unpack(inbox[phase, distance - 1, p])
            real = real + more[0]
            imag = imag + more[1]
        return real, imag

    pending = []
    for index in (1, 2, 4, 5, 0):
        loads[index].wait()
    for p in range(planes):
        sampled = mask[p].astype(jnp.float32)
        backward_part(measured[0, p] * sampled, measured[1, p] * sampled, 0, p)
        if p == 0:
            pl.semaphore_wait(barrier, devices - 1)
        pending.append(scatter(0, p))
    for index in (6, 8, 3, 7):
        loads[index].wait()
    first_weights(w_first, base, first_table)
    last_weights(w_last, last_table, last_table.shape[0] // 12)
    total = taken_fields.shape[2]
    for which in range(2):
        for outer in (0, total - 1):
            taken_fields[which, :, outer] = jnp.zeros((deep,) + taken_fields.shape[3:], jnp.float32)
    shifted[...] = jnp.zeros(shifted.shape, shifted.dtype)
    for buffer in (even, odd):
        for outer in (0, buffer.shape[1] - 1):
            buffer[:, outer] = jnp.zeros((buffer.shape[0],) + buffer.shape[2:], buffer.dtype)
    gathers = []
    norm = jnp.zeros((8, width), jnp.float32)
    for p in range(planes):
        finish(pending[p])
        real, imag = reduced(0, p)
        real = real + LAMBDA * prior[0, p]
        imag = imag + LAMBDA * prior[1, p]
        outbox[2, p, :block] = pack(real, imag)
        gathers.append(gather(2, p))
        for h, value in enumerate((real, imag)):
            own_rhs[h, p] = value
            rhs[h, p, mine] = value
            fields[0, halo : halo + block, 2 * p + h] = value
            norm = norm + fold(value * value)
    edge_copies = send_edges(0)
    middle_weights(w_middle, middle_table, y_outs)
    energy = LAMBDA * norm
    pending = []
    for p in range(planes):
        finish(gathers[p])
        for distance in range(1, coils):
            source = rows_of(lax.rem(coil + coils - distance, coils))
            real, imag = unpack(inbox[2, distance - 1, p])
            rhs[0, p, source] = real
            rhs[1, p, source] = imag
        real, imag = forward(rhs[0, p], rhs[1, p], p)
        energy = energy + fold(real * real + imag * imag)
        backward_part(real, imag, 1, p)
        pending.append(scatter(1, p))
    write_note(0, [total_of(norm), total_of(energy)])
    first_notes = tell(0)
    field_copies = send_fields(0, edge_copies)
    gathers = []
    for p in range(planes):
        finish(pending[p])
        images = reduced(1, p)
        images = [images[h] + LAMBDA * own_rhs[h, p] for h in range(2)]
        outbox[3, p, :block] = pack(*images)
        if p < planes - 1:
            gathers.append(gather(3, p))
        for h in range(2):
            own_image[h, p] = images[h]
            fields[1, halo : halo + block, 2 * p + h] = images[h]
    edge_copies = send_edges(1)
    gathers.append(gather(3, planes - 1))
    first_notes.wait_recv()
    norm, curvature = read_notes(0, 2)
    step = norm / curvature
    norm_next = jnp.zeros((8, width), jnp.float32)
    cross = jnp.zeros((8, width), jnp.float32)
    for p in range(planes):
        for h in range(2):
            image = own_image[h, p]
            value = own_rhs[h, p] - step * image
            norm_next = norm_next + fold(value * value)
            cross = cross + fold(value * image)
    energy = LAMBDA * norm_next
    norm_next, cross = total_of(norm_next), total_of(cross)
    for p in range(planes):
        finish(gathers[p])
        for h in range(2):
            residual[h, mine] = own_rhs[h, p] - step * own_image[h, p]
        for distance in range(1, coils):
            source = rows_of(lax.rem(coil + coils - distance, coils))
            for h, value in enumerate(unpack(inbox[3, distance - 1, p])):
                residual[h, source] = rhs[h, p, source] - step * value
        real, imag = forward(residual[0], residual[1], p)
        energy = energy + fold(real * real + imag * imag)
        if p == 0:
            field_copies = field_copies + send_fields(1, edge_copies)
    write_note(1, [norm_next, total_of(energy), cross])
    last_notes = tell(1)
    finish(field_copies)
    last_notes.wait_recv()
    norm_next, energy, cross = read_notes(1, 3)
    ratio = norm_next / norm
    curvature = energy + 2.0 * ratio * cross + ratio * ratio * curvature
    step_next = norm_next / curvature
    share = step + step_next * (1.0 + ratio)
    share_image = -step_next * step
    across = lax.broadcasted_iota(jnp.int32, (4 * total, width), 1)
    for y in range(deep):
        line = share * taken_fields[0, y].reshape(4 * total, width)
        line = line + share_image * taken_fields[1, y].reshape(4 * total, width)
        line = line.astype(jnp.bfloat16).astype(jnp.float32)
        before = jnp.where(across == 0, 0.0, pltpu.roll(line, 1, 1))
        after = jnp.where(across == width - 1, 0.0, pltpu.roll(line, width - 1, 1))
        for group in range(shifted.shape[2] // width):
            span = slice(16 * group, 16 * group + 24)
            piece = jnp.concatenate([before[span], line[span], after[span], jnp.zeros((8, width), jnp.float32)], axis=0)
            shifted[y, :, group * width : (group + 1) * width] = piece.astype(jnp.bfloat16)
    for h in range(2):
        for p in range(planes):
            half[h, p] = 0.5 * (share * own_rhs[h, p] + share_image * own_image[h, p])
    top = coil * block + slab * rows
    left = layers - 1
    conv_first(first_table, shifted, even, rows + 2 * left, top - left, height)
    buffers = (even, odd)
    for layer in range(layers - 2):
        left = left - 1
        conv_middle(
            middle_table.at[layer], buffers[layer % 2], buffers[(layer + 1) % 2], rows + 2 * left, y_outs,
            top - left, height,
        )
    copies = []

    def give(index, other):
        if index < shares - 1:
            copies.append(
                send(
                    corrections.at[other], arrived.at[slab], back_send.at[index], back_recv.at[index], (other, coil)
                )
            )

    order = [lax.rem(slab + shares - 1 - index, shares) for index in range(shares)]
    conv_last(last_table, buffers[(layers - 2) % 2], corrections, rows, order, give)
    arrived[slab] = corrections[slab]
    for copy in sent:
        copy.wait_send()
    first_notes.wait_send()
    last_notes.wait_send()
    sent.clear()
    finish(copies)
    for copy in copies:
        copy.wait_send()
    for s in range(shares):
        span = slice(s * rows, (s + 1) * rows)
        for p in range(planes):
            for h in range(2):
                correction[h, p, span] = arrived[s, 2 * p + h, :rows]


def body(sensitivity, kspace, sampling, prior_image, w_first, w_middle, w_last):
    maps, measured = sensitivity[0], kspace[0]
    planes, height, width = sampling.shape
    block = prior_image.shape[2]
    shares = lax.axis_size("slab")
    coils = lax.axis_size("coil")
    rows = block // shares
    channels = w_first.shape[0]
    layers = w_middle.shape[0] + 2
    whole = shares * planes
    y_outs = 2 if rows % 2 == 0 else 1
    cosine, sine = dft_parts(height)
    high, low = halves(np.concatenate([cosine, sine]))
    y_table = np.concatenate([high, low], axis=1)
    cosine, sine = dft_parts(width)
    high, low = halves(np.block([[cosine, -sine], [sine, cosine]]))
    z_table = np.concatenate([high, low], axis=0)
    w_first = jnp.transpose(w_first, (2, 3, 4, 1, 0))
    w_middle = jnp.transpose(w_middle, (0, 3, 4, 5, 1, 2)).reshape(layers - 2, 3, 3, 3 * channels, channels)
    w_last = jnp.transpose(w_last, (2, 3, 4, 0, 1))
    image = (2, planes, height, width)
    brick = (2, planes, block, width)
    tall = rows + -rows % 8
    deep = rows + 2 * layers
    hidden = (rows + 2 * (layers - 1), whole + 2, channels, width)
    operands = (maps, measured, sampling, prior_image, y_table, z_table, w_first, w_middle, w_last)
    kernel = pl.pallas_call(
        functools.partial(step_kernel, shares, coils),
        out_shape=[pltpu.VMEM(brick, jnp.float32)] * 2,
        in_specs=[pl.BlockSpec(memory_space=pl.ANY)] * 9,
        out_specs=[pl.BlockSpec(memory_space=pltpu.VMEM)] * 2,
        scratch_shapes=[pltpu.VMEM(operand.shape, operand.dtype) for operand in operands]
        + [
            pltpu.SemaphoreType.DMA((len(operands),)),
            pltpu.VMEM((2,) + image, jnp.float32),
            pltpu.VMEM((4, planes, height, width), jnp.int32),
            pltpu.VMEM((4, coils - 1, planes, block, width), jnp.int32),
            pltpu.VMEM(brick, jnp.float32),
            pltpu.VMEM(image, jnp.float32),
            pltpu.VMEM(brick, jnp.float32),
            pltpu.VMEM((2, height, width), jnp.float32),
            pltpu.VMEM((2, 1, 128), jnp.float32),
            pltpu.VMEM((2, shares * coils - 1, 1, 128), jnp.float32),
            pltpu.VMEM((2, block + 2 * layers, 2 * planes, width), jnp.float32),
            pltpu.VMEM((2, deep, shares + 2, 2 * planes, width), jnp.float32),
            pltpu.VMEM((56, 128), jnp.float32),
            pltpu.VMEM((8 * channels, 256), jnp.bfloat16),
            pltpu.VMEM((layers - 2, 2 * y_outs * 3 * channels, (y_outs + 2) * 4 * channels), jnp.bfloat16),
            pltpu.VMEM((12 * tall, (rows + 2) * 4 * channels), jnp.bfloat16),
            pltpu.VMEM((deep, 80, whole // 8 * width), jnp.bfloat16),
            pltpu.VMEM(hidden, jnp.bfloat16),
            pltpu.VMEM(hidden, jnp.bfloat16),
            pltpu.VMEM((shares, 2 * planes, tall, width), jnp.float32),
            pltpu.VMEM((shares, 2 * planes, tall, width), jnp.float32),
            pltpu.SemaphoreType.DMA((4, planes, coils - 1)),
            pltpu.SemaphoreType.DMA((4, planes, coils - 1)),
            pltpu.SemaphoreType.DMA((2,)),
            pltpu.SemaphoreType.DMA((2,)),
            pltpu.SemaphoreType.DMA((2, 2)),
            pltpu.SemaphoreType.DMA((2, 2)),
            pltpu.SemaphoreType.DMA((2, shares - 1)),
            pltpu.SemaphoreType.DMA((2, shares - 1)),
            pltpu.SemaphoreType.DMA((shares - 1,)),
            pltpu.SemaphoreType.DMA((shares - 1,)),
        ],
        compiler_params=pltpu.CompilerParams(
            collective_id=0, has_side_effects=True, vmem_limit_bytes=56 * 1024 * 1024
        ),
    )
    half, correction = kernel(*operands)
    image = half + half
    return image, image + correction


def solution(mesh):
    placed = (
        P("coil", None, "slab", None, None),
        P("coil", None, "slab", None, None),
        P("slab", None, None),
        P(None, "slab", "coil", None),
        P(),
        P(),
        P(),
    )
    return jax.shard_map(
        body,
        mesh=mesh,
        in_specs=placed,
        out_specs=(P(None, "slab", "coil", None), P(None, "slab", "coil", None)),
        check_vma=False,
    )
```

```python
import functools

import jax
import jax.numpy as jnp
import numpy as np
from jax import lax
from jax.experimental import pallas as pl
from jax.experimental.pallas import tpu as pltpu
from jax.sharding import PartitionSpec as P

LAMBDA = 0.5
MESH = pl.DeviceIdType.MESH


def dft_parts(length):
    positions = np.arange(length)
    angles = 2.0 * np.pi / length * (positions[:, None] * positions[None, :] % length)
    return np.cos(angles) / np.sqrt(length), np.sin(angles) / np.sqrt(length)


def halves(table):
    table = table.astype(np.float32)
    high = table.astype(jnp.bfloat16)
    low = (table - high.astype(np.float32)).astype(jnp.bfloat16)
    return high, low


def split(values):
    high = values.astype(jnp.bfloat16)
    return high, (values - high.astype(jnp.float32)).astype(jnp.bfloat16)


def multiply(left, right):
    return jnp.dot(left, right, preferred_element_type=jnp.float32)


def transform(real, imag, y_table, z_table):
    rows, width = real.shape
    high, low = split(jnp.concatenate([real, imag], axis=1))
    y_high, y_low = y_table[:, :rows], y_table[:, rows:]
    z_high, z_low = z_table[: 2 * width], z_table[2 * width :]
    field = multiply(
        jnp.concatenate([y_high, y_high, y_low], axis=1), jnp.concatenate([high, low, high], axis=0)
    )
    field = jnp.concatenate(
        [field[:rows, :width] + field[rows:, width:], field[:rows, width:] - field[rows:, :width]], axis=1
    )
    high, low = split(field)
    field = multiply(
        jnp.concatenate([high, low, high], axis=1), jnp.concatenate([z_high, z_high, z_low], axis=0)
    )
    return field[:, :width], field[:, width:]


def fold(values):
    return jnp.sum(values.reshape(values.shape[0] // 8, 8, values.shape[1]), axis=0)


def total_of(values):
    return jnp.sum(jnp.sum(values, axis=0, keepdims=True), axis=1, keepdims=True)


BIAS = 128
LOW_HALF = 65535


def pack(real, imag):
    largest = jnp.maximum(
        jnp.max(jnp.abs(real), axis=0, keepdims=True), jnp.max(jnp.abs(imag), axis=0, keepdims=True)
    )
    exponent = jnp.maximum(jnp.ceil(jnp.log2(jnp.maximum(largest, 1e-35)) - 14.98), -110.0)
    scale = jnp.exp2(-exponent)
    real = jnp.round(real * scale).astype(jnp.int32)
    imag = jnp.round(imag * scale).astype(jnp.int32)
    code = exponent.astype(jnp.int32) + BIAS
    places = lax.broadcasted_iota(jnp.int32, (8, real.shape[1]), 0)
    bits = jnp.bitwise_and(jnp.right_shift(jnp.broadcast_to(code, places.shape), places), 1)
    head = jnp.bitwise_or(jnp.bitwise_and(real[:8], -2), bits)
    real = jnp.concatenate([head, real[8:]], axis=0)
    return jnp.bitwise_or(jnp.left_shift(real, 16), jnp.bitwise_and(imag, LOW_HALF))


def unpack(words):
    real = jnp.right_shift(words, 16)
    imag = jnp.right_shift(jnp.left_shift(words, 16), 16)
    places = lax.broadcasted_iota(jnp.int32, (8, words.shape[1]), 0)
    bits = jnp.left_shift(jnp.bitwise_and(real[:8], 1), places)
    code = jnp.sum(bits, axis=0, keepdims=True)
    scale = jnp.exp2((code - BIAS).astype(jnp.float32))
    return real.astype(jnp.float32) * scale, imag.astype(jnp.float32) * scale


def spread(blocks, x_out):
    empty = jnp.zeros_like(blocks[0])
    return jnp.concatenate([empty] * x_out + blocks + [empty] * (1 - x_out), axis=1)


def first_weights(taps, base, table):
    outs = taps.shape[-1]
    for u in range(3):
        for v in range(3):
            for t in range(3):
                index = ((v * 3 + t) * 3 + u) * 2
                base[index : index + 2, :outs] = taps[u, v, t].astype(jnp.float32)
    window = (24, table.shape[0])
    row = lax.broadcasted_iota(jnp.int32, window, 0)
    place = row - 2 * (lax.broadcasted_iota(jnp.int32, window, 1) // outs) - 2
    rest = jnp.zeros((8, window[1]), jnp.float32)
    blocks = []
    for v in range(3):
        for t in range(3):
            block = jnp.zeros(window, jnp.float32)
            for k in range(6):
                index = (v * 3 + t) * 6 + k
                line = jnp.concatenate([base[index : index + 1, :outs]] * (window[1] // outs), axis=1)
                block = jnp.where(place == k, line, block)
            blocks.append(block)
        blocks.append(rest)
    blocks.append(jnp.zeros((16, window[1]), jnp.float32))
    table[...] = jnp.transpose(jnp.concatenate(blocks, axis=0)).astype(table.dtype)


def middle_weights(taps, table, y_outs):
    count, channels = taps.shape[3:]
    span = 4 * channels
    table[...] = jnp.zeros(table.shape, table.dtype)
    for layer in range(taps.shape[0]):
        for v in range(3):
            for x_out in range(2):
                block = spread([taps[layer, u, v] for u in range(3)], x_out)
                for y_out in range(y_outs):
                    base = (x_out * y_outs + y_out) * count
                    y_in = y_out + v
                    table[layer, base : base + count, y_in * span : (y_in + 1) * span] = block


def last_weights(taps, table, tall):
    channels = taps.shape[-1]
    span = 4 * channels
    row = lax.broadcasted_iota(jnp.int32, (tall, span), 0)
    for t in range(3):
        for x_out in range(2):
            lines = [spread([taps[u, v, t].astype(jnp.float32) for u in range(3)], x_out) for v in range(3)]
            for o in range(2):
                base = ((t * 2 + x_out) * 2 + o) * tall
                for y_in in range(table.shape[1] // span):
                    block = jnp.zeros((tall, span), jnp.float32)
                    for v in range(3):
                        block = jnp.where(row == y_in - v, lines[v][o : o + 1], block)
                    table[base : base + tall, y_in * span : (y_in + 1) * span] = block.astype(table.dtype)


def along_z(before, centre, after, lanes):
    width = centre.shape[1]
    before = jnp.where(lanes == 0, 0.0, pltpu.roll(before, 1, 1))
    after = jnp.where(lanes == width - 1, 0.0, pltpu.roll(after, width - 1, 1))
    return centre + before + after


def conv_first(table, taken, sink, rows, top, height):
    outs = sink.shape[2]
    width = sink.shape[3]
    depth = 3 * taken.shape[1]
    for y in range(rows):
        inside = jnp.logical_and(top + y >= 0, top + y < height)
        product = multiply(table[:, :depth], taken[y : y + 3].reshape(depth, taken.shape[2]))
        for group in range(taken.shape[2] // width):
            for q in range(table.shape[0] // outs):
                value = product[q * outs : (q + 1) * outs, group * width : (group + 1) * width]
                value = jnp.where(inside, jnp.maximum(value, 0.0), 0.0)
                sink[y, group * (table.shape[0] // outs) + q + 1] = value.astype(jnp.bfloat16)


def conv_middle(table, source, sink, rows, y_outs, top, height):
    planes, outs, width = source.shape[1] - 2, source.shape[2], source.shape[3]
    lanes = lax.broadcasted_iota(jnp.int32, (outs, width), 1)
    depth = (y_outs + 2) * 4 * outs
    group = 2 if planes % 4 == 0 else 1
    for y in range(0, rows, y_outs):
        for first in range(0, planes, 2 * group):
            taken = [
                source[y : y + y_outs + 2, first + 2 * k : first + 2 * k + 4].reshape(depth, width)
                for k in range(group)
            ]
            product = multiply(table[...], jnp.concatenate(taken, axis=1))
            for x_out in range(2):
                for y_out in range(y_outs):
                    base = (x_out * y_outs + y_out) * 3 * outs
                    inside = jnp.logical_and(top + y + y_out >= 0, top + y + y_out < height)
                    for k in range(group):
                        parts = [
                            product[base + t * outs : base + (t + 1) * outs, k * width : (k + 1) * width]
                            for t in range(3)
                        ]
                        value = along_z(*parts, lanes)
                        value = jnp.where(inside, jnp.maximum(value, 0.0), 0.0)
                        sink[y + y_out, first + 2 * k + x_out + 1] = value.astype(jnp.bfloat16)


def conv_last(table, source, sink, rows, order, ready):
    channels, width = source.shape[2], source.shape[3]
    tall = table.shape[0] // 3
    lanes = lax.broadcasted_iota(jnp.int32, (tall, width), 1)
    depth = (rows + 2) * 4 * channels
    for first in range(0, len(order), 2):
        targets = order[first : first + 2]
        taken = [source[: rows + 2, pl.ds(2 * target, 4)].reshape(depth, width) for target in targets]
        product = multiply(table[...], jnp.concatenate(taken, axis=1))
        for k, target in enumerate(targets):
            parts = [product[t * tall : (t + 1) * tall, k * width : (k + 1) * width] for t in range(3)]
            sink[target] = along_z(*parts, lanes).reshape(sink.shape[1:])
        for k, target in enumerate(targets):
            ready(first + k, target)


def step_kernel(
    shares, coils, *refs,
):
    outside, (half, correction), refs = refs[:9], refs[9:11], refs[11:]
    inside, load_sem, refs = refs[:9], refs[9], refs[10:]
    maps, measured, mask, prior, y_table, z_table, w_first, w_middle, w_last = inside
    (
        part, outbox, inbox, own_rhs, rhs, own_image, residual, note, notes, fields, taken_fields,
        base, first_table, middle_table, last_table, shifted, even, odd, corrections, arrived,
        block_send, block_recv, note_send, note_recv, edge_send, edge_recv, field_send, field_recv, back_send, back_recv,
    ) = refs
    loads = [
        pltpu.make_async_copy(source, target, load_sem.at[index])
        for index, (source, target) in enumerate(zip(outside, inside))
    ]
    slab = lax.axis_index("slab")
    coil = lax.axis_index("coil")
    devices = shares * coils
    planes = maps.shape[1]
    height, width = maps.shape[2:]
    block = prior.shape[2]
    rows = block // shares
    layers = w_middle.shape[0] + 2
    halo = layers
    y_outs = 2 if rows % 2 == 0 else 1
    tables = (y_table, z_table)

    offsets = [(s, c) for s in range(shares) for c in range(coils) if s or c]
    offsets.sort(key=lambda offset: -min(offset[1], coils - offset[1]) - bin(offset[0] // 2).count("1"))

    def device_at(distance):
        far_slab, far_coil = offsets[distance - 1]
        return (lax.rem(slab + far_slab, shares), lax.rem(coil + far_coil, coils))

    barrier = pltpu.get_barrier_semaphore()
    for distance in range(1, devices):
        pl.semaphore_signal(barrier, inc=1, device_id=device_at(distance), device_id_type=MESH)

    for index in (1, 2, 4, 5, 0, 6, 8, 3, 7):
        loads[index].start()

    def rows_of(index):
        return pl.ds(pl.multiple_of(index * block, block), block)

    mine = rows_of(coil)

    def send(source, target, send_sem, recv_sem, device):
        copy = pltpu.make_async_remote_copy(
            src_ref=source, dst_ref=target, send_sem=send_sem, recv_sem=recv_sem,
            device_id=device, device_id_type=MESH,
        )
        copy.start()
        return copy

    def to_coils(phase, p, source, target):
        copies = []
        for distance in range(1, coils):
            other = lax.rem(coil + distance, coils)
            copies.append(
                send(
                    source(other), target(distance), block_send.at[phase, p, distance - 1],
                    block_recv.at[phase, p, distance - 1], (slab, other),
                )
            )
        return copies

    def scatter(phase, p):
        return to_coils(
            phase, p, lambda other: outbox.at[phase, p, rows_of(other)],
            lambda distance: inbox.at[phase, distance - 1, p],
        )

    def gather(phase, p):
        return to_coils(
            phase, p, lambda other: outbox.at[phase, p, pl.ds(0, block)],
            lambda distance: inbox.at[phase, distance - 1, p],
        )

    def tell(phase):
        for distance in range(1, devices):
            send(
                note.at[phase], notes.at[phase, distance - 1], note_send.at[phase], note_recv.at[phase],
                device_at(distance),
            )
        return pltpu.make_async_remote_copy(
            src_ref=notes.at[phase], dst_ref=notes.at[phase], send_sem=note_send.at[phase],
            recv_sem=note_recv.at[phase], device_id=device_at(1), device_id_type=MESH,
        )

    def send_edges(which):
        above = lax.rem(coil + coils - 1, coils)
        below = lax.rem(coil + 1, coils)
        ends = ((block, 0, below), (halo, halo + block, above))
        return [
            send(
                fields.at[which, pl.ds(source, halo)], fields.at[which, pl.ds(target, halo)],
                edge_send.at[which, side], edge_recv.at[which, side], (slab, other),
            )
            for side, (source, target, other) in enumerate(ends)
        ]

    deep = rows + 2 * halo

    def send_fields(which, copies):
        finish(copies)
        top_edge = fields[which, :halo]
        fields[which, :halo] = jnp.where(coil > 0, top_edge, 0.0)
        low_edge = fields[which, halo + block :]
        fields[which, halo + block :] = jnp.where(coil < coils - 1, low_edge, 0.0)
        copies = []
        for distance in range(1, shares):
            other = lax.rem(slab + distance, shares)
            copies.append(
                send(
                    fields.at[which, pl.ds(other * rows, deep)], taken_fields.at[which, :, slab + 1],
                    field_send.at[which, distance - 1], field_recv.at[which, distance - 1], (other, coil),
                )
            )
        taken_fields[which, :, slab + 1] = fields[which, pl.ds(slab * rows, deep)]
        return copies

    sent = []

    def finish(copies):
        for copy in copies:
            copy.wait_recv()
        sent.extend(copies)

    lanes = lax.broadcasted_iota(jnp.int32, (1, note.shape[2]), 1)

    def write_note(phase, values):
        line = jnp.zeros(lanes.shape, jnp.float32)
        for index, value in enumerate(values):
            line = jnp.where(lanes == index, value, line)
        note[phase] = line

    def read_notes(phase, count):
        line = note[phase]
        for distance in range(1, devices):
            line = line + notes[phase, distance - 1]
        return [jnp.sum(jnp.where(lanes == index, line, 0.0), axis=1, keepdims=True) for index in range(count)]

    def backward_part(real, imag, phase, p):
        imag, real = transform(imag, real, *tables)
        part_re = maps[0, p] * real + maps[1, p] * imag
        part_im = maps[0, p] * imag - maps[1, p] * real
        part[phase, 0, p] = part_re
        part[phase, 1, p] = part_im
        for index in range(coils):
            span = slice(index * block, (index + 1) * block)
            outbox[phase, p, span] = pack(part_re[span], part_im[span])

    def forward(image_re, image_im, p):
        real = maps[0, p] * image_re - maps[1, p] * image_im
        imag = maps[0, p] * image_im + maps[1, p] * image_re
        real, imag = transform(real, imag, *tables)
        sampled = mask[p].astype(jnp.float32)
        return real * sampled, imag * sampled

    def reduced(phase, p):
        real = part[phase, 0, p, mine]
        imag = part[phase, 1, p, mine]
        for distance in range(1, coils):
            more = unpack(inbox[phase, distance - 1, p])
            real = real + more[0]
            imag = imag + more[1]
        return real, imag

    pending = []
    for index in (1, 2, 4, 5, 0):
        loads[index].wait()
    for p in range(planes):
        sampled = mask[p].astype(jnp.float32)
        backward_part(measured[0, p] * sampled, measured[1, p] * sampled, 0, p)
        if p == 0:
            pl.semaphore_wait(barrier, devices - 1)
        pending.append(scatter(0, p))
    for index in (6, 8, 3, 7):
        loads[index].wait()
    first_weights(w_first, base, first_table)
    last_weights(w_last, last_table, last_table.shape[0] // 12)
    total = taken_fields.shape[2]
    for which in range(2):
        for outer in (0, total - 1):
            taken_fields[which, :, outer] = jnp.zeros((deep,) + taken_fields.shape[3:], jnp.float32)
    shifted[...] = jnp.zeros(shifted.shape, shifted.dtype)
    for buffer in (even, odd):
        for outer in (0, buffer.shape[1] - 1):
            buffer[:, outer] = jnp.zeros((buffer.shape[0],) + buffer.shape[2:], buffer.dtype)
    gathers = []
    norm = jnp.zeros((8, width), jnp.float32)
    for p in range(planes):
        finish(pending[p])
        real, imag = reduced(0, p)
        real = real + LAMBDA * prior[0, p]
        imag = imag + LAMBDA * prior[1, p]
        outbox[2, p, :block] = pack(real, imag)
        gathers.append(gather(2, p))
        for h, value in enumerate((real, imag)):
            own_rhs[h, p] = value
            rhs[h, p, mine] = value
            fields[0, halo : halo + block, 2 * p + h] = value
            norm = norm + fold(value * value)
    edge_copies = send_edges(0)
    middle_weights(w_middle, middle_table, y_outs)
    energy = LAMBDA * norm
    pending = []
    for p in range(planes):
        finish(gathers[p])
        for distance in range(1, coils):
            source = rows_of(lax.rem(coil + coils - distance, coils))
            real, imag = unpack(inbox[2, distance - 1, p])
            rhs[0, p, source] = real
            rhs[1, p, source] = imag
        real, imag = forward(rhs[0, p], rhs[1, p], p)
        energy = energy + fold(real * real + imag * imag)
        backward_part(real, imag, 1, p)
        pending.append(scatter(1, p))
    write_note(0, [total_of(norm), total_of(energy)])
    first_notes = tell(0)
    field_copies = send_fields(0, edge_copies)
    gathers = []
    for p in range(planes):
        finish(pending[p])
        images = reduced(1, p)
        images = [images[h] + LAMBDA * own_rhs[h, p] for h in range(2)]
        outbox[3, p, :block] = pack(*images)
        if p < planes - 1:
            gathers.append(gather(3, p))
        for h in range(2):
            own_image[h, p] = images[h]
            fields[1, halo : halo + block, 2 * p + h] = images[h]
    edge_copies = send_edges(1)
    gathers.append(gather(3, planes - 1))
    first_notes.wait_recv()
    norm, curvature = read_notes(0, 2)
    step = norm / curvature
    norm_next = jnp.zeros((8, width), jnp.float32)
    cross = jnp.zeros((8, width), jnp.float32)
    for p in range(planes):
        for h in range(2):
            image = own_image[h, p]
            value = own_rhs[h, p] - step * image
            norm_next = norm_next + fold(value * value)
            cross = cross + fold(value * image)
    energy = LAMBDA * norm_next
    norm_next, cross = total_of(norm_next), total_of(cross)
    for p in range(planes):
        finish(gathers[p])
        if p == 0:
            field_copies = field_copies + send_fields(1, edge_copies)
        for h in range(2):
            residual[h, mine] = own_rhs[h, p] - step * own_image[h, p]
        for distance in range(1, coils):
            source = rows_of(lax.rem(coil + coils - distance, coils))
            for h, value in enumerate(unpack(inbox[3, distance - 1, p])):
                residual[h, source] = rhs[h, p, source] - step * value
        real, imag = forward(residual[0], residual[1], p)
        energy = energy + fold(real * real + imag * imag)
    write_note(1, [norm_next, total_of(energy), cross])
    last_notes = tell(1)
    finish(field_copies)
    last_notes.wait_recv()
    norm_next, energy, cross = read_notes(1, 3)
    ratio = norm_next / norm
    curvature = energy + 2.0 * ratio * cross + ratio * ratio * curvature
    step_next = norm_next / curvature
    share = step + step_next * (1.0 + ratio)
    share_image = -step_next * step
    across = lax.broadcasted_iota(jnp.int32, (4 * total, width), 1)
    for y in range(deep):
        line = share * taken_fields[0, y].reshape(4 * total, width)
        line = line + share_image * taken_fields[1, y].reshape(4 * total, width)
        line = line.astype(jnp.bfloat16).astype(jnp.float32)
        before = jnp.where(across == 0, 0.0, pltpu.roll(line, 1, 1))
        after = jnp.where(across == width - 1, 0.0, pltpu.roll(line, width - 1, 1))
        for group in range(shifted.shape[2] // width):
            span = slice(16 * group, 16 * group + 24)
            piece = jnp.concatenate([before[span], line[span], after[span], jnp.zeros((8, width), jnp.float32)], axis=0)
            shifted[y, :, group * width : (group + 1) * width] = piece.astype(jnp.bfloat16)
    for h in range(2):
        for p in range(planes):
            half[h, p] = 0.5 * (share * own_rhs[h, p] + share_image * own_image[h, p])
    top = coil * block + slab * rows
    left = layers - 1
    conv_first(first_table, shifted, even, rows + 2 * left, top - left, height)
    buffers = (even, odd)
    for layer in range(layers - 2):
        left = left - 1
        conv_middle(
            middle_table.at[layer], buffers[layer % 2], buffers[(layer + 1) % 2], rows + 2 * left, y_outs,
            top - left, height,
        )
    copies = []

    def give(index, other):
        if index < shares - 1:
            copies.append(
                send(
                    corrections.at[other], arrived.at[slab], back_send.at[index], back_recv.at[index], (other, coil)
                )
            )

    order = [lax.rem(slab + shares - 1 - index, shares) for index in range(shares)]
    conv_last(last_table, buffers[(layers - 2) % 2], corrections, rows, order, give)
    arrived[slab] = corrections[slab]
    for copy in sent:
        copy.wait_send()
    first_notes.wait_send()
    last_notes.wait_send()
    sent.clear()
    finish(copies)
    for copy in copies:
        copy.wait_send()
    for s in range(shares):
        span = slice(s * rows, (s + 1) * rows)
        for p in range(planes):
            for h in range(2):
                correction[h, p, span] = arrived[s, 2 * p + h, :rows]


def body(sensitivity, kspace, sampling, prior_image, w_first, w_middle, w_last):
    maps, measured = sensitivity[0], kspace[0]
    planes, height, width = sampling.shape
    block = prior_image.shape[2]
    shares = lax.axis_size("slab")
    coils = lax.axis_size("coil")
    rows = block // shares
    channels = w_first.shape[0]
    layers = w_middle.shape[0] + 2
    whole = shares * planes
    y_outs = 2 if rows % 2 == 0 else 1
    cosine, sine = dft_parts(height)
    high, low = halves(np.concatenate([cosine, sine]))
    y_table = np.concatenate([high, low], axis=1)
    cosine, sine = dft_parts(width)
    high, low = halves(np.block([[cosine, -sine], [sine, cosine]]))
    z_table = np.concatenate([high, low], axis=0)
    w_first = jnp.transpose(w_first, (2, 3, 4, 1, 0))
    w_middle = jnp.transpose(w_middle, (0, 3, 4, 5, 1, 2)).reshape(layers - 2, 3, 3, 3 * channels, channels)
    w_last = jnp.transpose(w_last, (2, 3, 4, 0, 1))
    image = (2, planes, height, width)
    brick = (2, planes, block, width)
    tall = rows + -rows % 8
    deep = rows + 2 * layers
    hidden = (rows + 2 * (layers - 1), whole + 2, channels, width)
    operands = (maps, measured, sampling, prior_image, y_table, z_table, w_first, w_middle, w_last)
    kernel = pl.pallas_call(
        functools.partial(step_kernel, shares, coils),
        out_shape=[pltpu.VMEM(brick, jnp.float32)] * 2,
        in_specs=[pl.BlockSpec(memory_space=pl.ANY)] * 9,
        out_specs=[pl.BlockSpec(memory_space=pltpu.VMEM)] * 2,
        scratch_shapes=[pltpu.VMEM(operand.shape, operand.dtype) for operand in operands]
        + [
            pltpu.SemaphoreType.DMA((len(operands),)),
            pltpu.VMEM((2,) + image, jnp.float32),
            pltpu.VMEM((4, planes, height, width), jnp.int32),
            pltpu.VMEM((4, coils - 1, planes, block, width), jnp.int32),
            pltpu.VMEM(brick, jnp.float32),
            pltpu.VMEM(image, jnp.float32),
            pltpu.VMEM(brick, jnp.float32),
            pltpu.VMEM((2, height, width), jnp.float32),
            pltpu.VMEM((2, 1, 128), jnp.float32),
            pltpu.VMEM((2, shares * coils - 1, 1, 128), jnp.float32),
            pltpu.VMEM((2, block + 2 * layers, 2 * planes, width), jnp.float32),
            pltpu.VMEM((2, deep, shares + 2, 2 * planes, width), jnp.float32),
            pltpu.VMEM((56, 128), jnp.float32),
            pltpu.VMEM((8 * channels, 256), jnp.bfloat16),
            pltpu.VMEM((layers - 2, 2 * y_outs * 3 * channels, (y_outs + 2) * 4 * channels), jnp.bfloat16),
            pltpu.VMEM((12 * tall, (rows + 2) * 4 * channels), jnp.bfloat16),
            pltpu.VMEM((deep, 80, whole // 8 * width), jnp.bfloat16),
            pltpu.VMEM(hidden, jnp.bfloat16),
            pltpu.VMEM(hidden, jnp.bfloat16),
            pltpu.VMEM((shares, 2 * planes, tall, width), jnp.float32),
            pltpu.VMEM((shares, 2 * planes, tall, width), jnp.float32),
            pltpu.SemaphoreType.DMA((4, planes, coils - 1)),
            pltpu.SemaphoreType.DMA((4, planes, coils - 1)),
            pltpu.SemaphoreType.DMA((2,)),
            pltpu.SemaphoreType.DMA((2,)),
            pltpu.SemaphoreType.DMA((2, 2)),
            pltpu.SemaphoreType.DMA((2, 2)),
            pltpu.SemaphoreType.DMA((2, shares - 1)),
            pltpu.SemaphoreType.DMA((2, shares - 1)),
            pltpu.SemaphoreType.DMA((shares - 1,)),
            pltpu.SemaphoreType.DMA((shares - 1,)),
        ],
        compiler_params=pltpu.CompilerParams(
            collective_id=0, has_side_effects=True, vmem_limit_bytes=56 * 1024 * 1024
        ),
    )
    half, correction = kernel(*operands)
    image = half + half
    return image, image + correction


def solution(mesh):
    placed = (
        P("coil", None, "slab", None, None),
        P("coil", None, "slab", None, None),
        P("slab", None, None),
        P(None, "slab", "coil", None),
        P(),
        P(),
        P(),
    )
    return jax.shard_map(
        body,
        mesh=mesh,
        in_specs=placed,
        out_specs=(P(None, "slab", "coil", None), P(None, "slab", "coil", None)),
        check_vma=False,
    )
```
